512 devices in a mesh: req: 32 (over z_hi, x, core), seq: 16 (over z_lo, y).
Axes of the slice: x: 4, y: 8, z: 8 (z_hi: 4, z_lo: 2; z = z_hi * 2 + z_lo), core: 2. Of those that a mesh axis runs over, the one named last changes fastest.
Arguments:
- layer_input: bfloat16 [32, 256, 2048], P('req', 'seq'), may hold values from -3 to 3
- queries: bfloat16 [32, 256, 4096], P('req', 'seq'), may hold values from -4.5 to 4.5
- fresh_kv: bfloat16 [32, 256, 1024], P('req', 'seq'), may hold values from -4.5 to 4.5
- cache_kv: bfloat16 [32, 1792, 1024], P('req', 'seq'), may hold values from -4.5 to 4.5
- cached_len: int32 [32], P('req'), may hold values from 2 to 1792, as said below
- out_weight: bfloat16 [4096, 2048], P('seq', 'req'), may hold values from -0.09375 to 0.09375
- norm_gain: float32 [2048], replicated, may hold values from 0.5 to 1.5
- routes: int32 [32, 256, 8], P('req', 'seq'), may hold values from 0 to 127, all different within a row; in each aligned block of 16 rows (0 to 15, 16 to 31, ..., all dimensions but the last counted through in order) at most 2 rows name the same one
- route_gates: float32 [32, 256, 8], P('req', 'seq'), may hold values from 0.2 to 1
- w_gate_up: bfloat16 [512, 2048, 384], P(('req', 'seq')), may hold values from -0.125 to 0.125
- w_down: bfloat16 [512, 192, 2048], P(('req', 'seq')), may hold values from -0.21875 to 0.21875
Outputs:
- output: bfloat16 [32, 256, 2048], P('req', 'seq')
The draws below stay inside these ranges and needn't reach their ends.
Inputs may be any that keep to these rules, and one draw needn't show every extreme that they name: Request r has cached_len[r] valid cached rows; some request has exactly 1792. `routes`: each token names 8 different experts; among the 16 tokens of one device (aligned blocks), no expert is named more than 2 times.
All inputs are finite; a program needn't handle non-finite values.
Results may differ from the reference program's by a relative error of at most 0.03.
Values may be sent and summed in bfloat16 or wider, within the bound.
A program may use at most 64 MiB of HBM per device.

```python
import math
import jax
import jax.numpy as jnp
import numpy as np
from jax import lax

D = 2048
QH = 32
KVH = 4
HD = 128
EXPERTS = 128
FF = 768
TOP = 8
NEW_DEV = 16
CAP = 2
REQS = 32
SPAN = 256
CACHE = 1792
SPLIT = 4
SLABS = 512
FFS = 192


def draw_queries(key, part):
    base_key = jax.random.fold_in(key, 11)
    base = jnp.clip(1.5 * jax.random.normal(base_key, (REQS, SPAN, QH * HD), jnp.float32), -4.5, 4.5)
    return base.astype(jnp.bfloat16)


def draw_cache_kv(key, part):
    base_key = jax.random.fold_in(key, 31)
    base = jnp.clip(jax.random.normal(base_key, (REQS, CACHE, 2 * KVH * HD), jnp.float32), -4.5, 4.5)
    return base.astype(jnp.bfloat16)


def draw_cached_len(key, part):
    lengths_drawn = jax.random.randint(jax.random.fold_in(key, 21), (REQS,), 2, CACHE + 1)
    longest = jax.random.randint(jax.random.fold_in(key, 22), (), 0, REQS)
    return lengths_drawn.at[longest].set(CACHE).astype(jnp.int32)


def block_levels(own_key, shape, split, low, high):
    def one(dim, shards_of):
        draws = jax.random.uniform(jax.random.fold_in(jax.random.fold_in(own_key, 6), dim), (shards_of,), jnp.float32, low / len(split), high / len(split))
        return jnp.repeat(jnp.exp(draws), shape[dim] // shards_of).reshape((-1,) + (1,) * (len(shape) - dim - 1))

    gain = one(*split[0])
    for cut in split[1:]:
        gain = gain * one(*cut)
    return gain


def shared_out(own_key, own, number, rows, number_of, top, most, slope):
    sequence = jax.random.permutation(own_key, number_of)
    crowded, ordinary = portions_of(number_of, rows * top, most, slope, True), portions_of(number_of, rows * top, most, slope, False)
    places = jnp.arange(number_of)

    def named(sizes, turn):
        used = int((sizes > 0).sum())
        fixed = max(1, used // 4)
        shifted = fixed + (places - fixed + turn * (used - fixed)) % max(1, number_of - fixed)
        return jnp.zeros((number_of,), jnp.int32).at[sequence[jnp.where(places < fixed, places, shifted)]].set(jnp.asarray(sizes, jnp.int32))

    sizes = jnp.where(number % 4 == 0, named(crowded, number // 4), named(ordinary, number - number // 4 - 1))
    mixed = jax.random.permutation(jax.random.fold_in(own, 3), number_of)
    giver, receiver = mixed[0:number_of // 2 * 2:2], mixed[1:number_of // 2 * 2:2]
    room = jnp.minimum(sizes[giver] - 1, most - sizes[receiver]) // 2
    room = jnp.where((giver == sequence[0]) | (receiver == sequence[0]) | (sizes[receiver] == 0), 0, jnp.maximum(room, 0))
    shifted = jax.random.randint(jax.random.fold_in(own, 4), (number_of // 2,), 0, 1 << 20) % (room + 1)
    sizes = sizes.at[giver].add(-shifted).at[receiver].add(shifted)
    members = jnp.searchsorted(jnp.cumsum(sizes), jnp.arange(rows * top), side="right").astype(jnp.int32)
    table = members.reshape(top, rows).T
    table = table[jax.random.permutation(jax.random.fold_in(own, 1), rows)]
    turn = jax.random.randint(jax.random.fold_in(own, 2), (rows, 1), 0, top)
    return jnp.take_along_axis(table, (jnp.arange(top)[None, :] + turn) % top, axis=1)


def portions_of(number_of, total, bound, lean, full):
    portions = [(1 << 20) // math.isqrt(standing ** lean) + 1 for standing in range(1, number_of + 1)]
    largest = bound if full else min(bound, max(-(-total // number_of), total * portions[0] // sum(portions)))
    least = 1 if total - largest >= number_of - 1 else 0
    holding, spare = [largest] + [least] * (number_of - 1), total - largest - least * (number_of - 1)
    while spare > 0:
        movable = [i for i in range(1, number_of) if holding[i] < largest] or [i for i in range(1, number_of) if holding[i] < bound]
        mass, left = sum([portions[i] for i in movable]), spare
        for i in movable:
            addition = min(bound - holding[i], max(1, left * portions[i] // mass), spare)
            holding[i] = holding[i] + addition
            spare = spare - addition
    return np.array(holding)


def gaussian(rng, extent, width, reach, pieces=(), kind=jnp.bfloat16):
    values = jax.random.normal(rng, extent, jnp.float32) * width
    if len(pieces) > 0:
        values = block_levels(rng, extent, pieces, -0.22, 0.18) * values
    return jnp.clip(values, min=-reach, max=reach).astype(kind)


def setup_inputs(seed: int = 0) -> dict:
    arg_keys = jax.random.split(jax.random.key(seed), 12)
    layer_input = gaussian(arg_keys[0], (REQS, SPAN, D), 0.5, 3.0, ((0, 32), (1, 16)))
    queries = draw_queries(jax.random.fold_in(arg_keys[11], 71), 0)
    fresh_kv = gaussian(arg_keys[2], (REQS, SPAN, 2 * KVH * HD), 1.0, 4.5, ((0, 32), (1, 16)))
    cache_kv = draw_cache_kv(jax.random.fold_in(arg_keys[11], 71), 0)
    cached_len = draw_cached_len(jax.random.fold_in(arg_keys[11], 71), 0)
    out_weight = gaussian(arg_keys[5], (QH * HD, D), (QH * HD) ** -0.5, 0.09375, ((0, 16), (1, 32)))
    norm_gain = jnp.clip(1.0 + 0.1 * jax.random.normal(arg_keys[6], (D,), jnp.float32), 0.5, 1.5)
    routes_keys = jax.random.split(jax.random.fold_in(arg_keys[7], 1), REQS * SPAN // NEW_DEV)
    routes_turns = jax.random.permutation(jax.random.fold_in(arg_keys[7], 3), REQS * SPAN // NEW_DEV)
    routes = jax.vmap(lambda own, number: shared_out(jax.random.fold_in(arg_keys[7], 2), own, number, NEW_DEV, EXPERTS, TOP, CAP, 2))(routes_keys, routes_turns).reshape((REQS, SPAN, TOP))
    route_gates = jnp.clip(0.2 + 0.8 * jax.random.uniform(arg_keys[8], (REQS, SPAN, TOP), jnp.float32) ** block_levels(arg_keys[8], (REQS, SPAN, TOP), ((0, 32), (1, 16)), -0.2, 0.2), 0.2, 1.0)
    w_gate_up = gaussian(arg_keys[9], (SLABS, D, 2 * FFS), D ** -0.5, 0.125, ((0, 512),))
    w_down = gaussian(arg_keys[10], (SLABS, FFS, D), FF ** -0.5, 0.21875, ((0, 512),))
    return {"layer_input": layer_input, "queries": queries, "fresh_kv": fresh_kv, "cache_kv": cache_kv, "cached_len": cached_len, "out_weight": out_weight, "norm_gain": norm_gain, "routes": routes, "route_gates": route_gates, "w_gate_up": w_gate_up, "w_down": w_down}


neg_large = -1e+30
epsilon = 1e-06

def reference(layer_input, queries, fresh_kv, cache_kv, cached_len, out_weight, norm_gain, routes, route_gates, w_gate_up, w_down):
    group_size = QH // KVH
    kv_width = KVH * HD
    scale = 1.0 / math.sqrt(HD)

    def one_request(packed):
        query_rows, cache_rows, fresh_rows, length = packed
        keyvals = jnp.concatenate([cache_rows, fresh_rows], 0)
        key_part = keyvals[:, :kv_width].reshape(CACHE + SPAN, KVH, HD).astype(jnp.float32)
        value_part = keyvals[:, kv_width:].reshape(CACHE + SPAN, KVH, HD).astype(jnp.float32)
        grouped = query_rows.reshape(SPAN, KVH, group_size, HD).astype(jnp.float32)
        scores = jnp.einsum('ngqc,pgc->ngqp', grouped, key_part, precision=lax.Precision.HIGHEST) * scale
        position = jnp.arange(CACHE + SPAN, dtype=jnp.int32)
        query_at = jnp.arange(SPAN, dtype=jnp.int32)
        visible = jnp.where((position < CACHE)[None, :], (position < length)[None, :], (position - CACHE)[None, :] <= query_at[:, None])
        mask = visible[:, None, None, :]
        scores = jnp.where(mask, scores, neg_large)
        running_max = lax.optimization_barrier(jnp.max(scores, axis=-1, keepdims=True))
        weights = jnp.where(mask, jnp.exp(scores - running_max), 0.0)
        denominator = lax.optimization_barrier(jnp.sum(weights, axis=-1))
        probs = lax.optimization_barrier(weights.astype(jnp.bfloat16)).astype(jnp.float32)
        mixed_values = jnp.einsum('ngqp,pgc->ngqc', probs, value_part, precision=lax.Precision.HIGHEST)
        return (mixed_values / denominator[..., None]).reshape(SPAN, QH * HD).astype(jnp.bfloat16)
    attended = lax.map(one_request, (queries, cache_kv, fresh_kv, cached_len))
    token_total = REQS * SPAN
    projected = jnp.dot(attended.reshape(token_total, QH * HD), out_weight, preferred_element_type=jnp.float32)
    residual = (layer_input.reshape(token_total, D).astype(jnp.float32) + projected).astype(jnp.bfloat16)
    residual_f = residual.astype(jnp.float32)
    normed = (residual_f * lax.rsqrt(lax.optimization_barrier(jnp.mean(residual_f * residual_f, axis=-1, keepdims=True)) + epsilon) * norm_gain).astype(jnp.bfloat16)
    block_count = token_total // NEW_DEV
    pair_count = NEW_DEV * TOP
    chosen = routes.reshape(block_count, pair_count)
    onehot = (chosen[:, :, None] == jnp.arange(EXPERTS, dtype=jnp.int32)[None, None, :]).astype(jnp.int32)
    earlier = jnp.cumsum(onehot, axis=1) - onehot
    slot_at = lax.optimization_barrier(jnp.sum(earlier * onehot, axis=2))
    block_id = jnp.arange(block_count, dtype=jnp.int32)[:, None]
    target = ((chosen * block_count + block_id) * CAP + slot_at).reshape(-1).astype(jnp.int32)
    token_id = (block_id * NEW_DEV + jnp.arange(pair_count, dtype=jnp.int32)[None, :] // TOP).reshape(-1).astype(jnp.int32)
    slot_total = block_count * CAP
    table = jnp.full((EXPERTS * slot_total,), token_total, dtype=jnp.int32).at[target].set(token_id)
    gate_table = jnp.zeros((EXPERTS * slot_total,), jnp.float32).at[target].set(route_gates.reshape(-1).astype(jnp.float32))
    padded = jnp.concatenate([normed, jnp.zeros((1, D), jnp.bfloat16)], 0)

    def per_expert(mixture, expert):
        row_ids = lax.dynamic_slice_in_dim(table, (expert * slot_total).astype(jnp.int32), slot_total)
        gate_rows = lax.dynamic_slice_in_dim(gate_table, (expert * slot_total).astype(jnp.int32), slot_total)
        token_rows = padded[row_ids]
        summed = jnp.zeros((slot_total, D), jnp.float32)
        for part_index in range(SPLIT):
            slab_id = (expert * SPLIT + part_index).astype(jnp.int32)
            gate_up = lax.dynamic_index_in_dim(w_gate_up, slab_id, 0, keepdims=False)
            down_rows = lax.dynamic_index_in_dim(w_down, slab_id, 0, keepdims=False)
            both = jnp.dot(token_rows, gate_up, preferred_element_type=jnp.float32)
            hidden = (jax.nn.silu(both[:, :FFS]) * both[:, FFS:]).astype(jnp.bfloat16)
            part_out = lax.optimization_barrier(jnp.dot(hidden, down_rows, preferred_element_type=jnp.float32).astype(jnp.bfloat16))
            summed = summed + part_out.astype(jnp.float32)
        expert_out = lax.optimization_barrier(summed.astype(jnp.bfloat16)).astype(jnp.float32)
        mixture = mixture.at[row_ids].add(gate_rows[:, None] * expert_out)
        return (mixture, None)
    mixture, _ = lax.scan(per_expert, jnp.zeros((token_total + 1, D), jnp.float32), jnp.arange(EXPERTS, dtype=jnp.int32))
    output = (residual_f + mixture[:token_total]).astype(jnp.bfloat16)
    return output.reshape(REQS, SPAN, D)
```

```python
import math

import jax
import jax.numpy as jnp
from jax import lax
from jax.experimental import pallas as pl
from jax.experimental.pallas import tpu as pltpu
from jax.sharding import PartitionSpec as P

MESH = pl.DeviceIdType.MESH
BF = jnp.bfloat16
F32 = jnp.float32
NEG = -1e30
EPS = 1e-06
D = 2048
HD = 128
NT = (((1,), (1,)), ((), ()))


def coords():
    req, seq = lax.axis_index("req"), lax.axis_index("seq")
    z = (req // 8) * 2 + seq // 8
    return (req // 2) % 4, seq % 8, z, req % 2


def device(x, y, z, c):
    return ((z // 2) * 8 + x * 2 + c, (z % 2) * 8 + y)


def remote(src, dst, send, recv, dev):
    return pltpu.make_async_remote_copy(
        src_ref=src, dst_ref=dst, send_sem=send, recv_sem=recv, device_id=dev, device_id_type=MESH
    )


def greet(devs):
    barrier = pltpu.get_barrier_semaphore()
    for dev in devs:
        pl.semaphore_signal(barrier, inc=1, device_id=dev, device_id_type=MESH)
    pl.semaphore_wait(barrier, len(devs))


def attention_kernel(
    len_ref, kv_ref, q_ref, wt_ref, x_ref, gain_ref, res_ref, normed_ref,
    kbuf, vbuf, qbuf, wbuf, att, pbuf, rbuf,
    own_sem, kv_send, kv_recv, w_send, w_recv, sib_send, sib_recv, p_send, p_recv,
):
    req, seq = lax.axis_index("req"), lax.axis_index("seq")
    m, c = req // 2, req % 2
    peers = [(req, lax.rem(seq + i, 16)) for i in range(1, 16)]
    chips = [(lax.rem(m + i, 16) * 2 + c, seq) for i in range(1, 16)]
    sibling = (m * 2 + 1 - c, seq)
    greet(peers + chips + [sibling])

    def piece(part, dst_seq, src_seq, i):
        rows = pl.ds(pl.multiple_of(src_seq * 128, 128), 128)
        head = dst_seq // 4
        if part == 0:
            cols = pl.ds(pl.multiple_of(head * HD, HD), HD)
            return kv_ref.at[:, cols], kbuf.at[rows, :]
        if part == 1:
            cols = pl.ds(pl.multiple_of(512 + head * HD, HD), HD)
            return kv_ref.at[:, cols], vbuf.at[rows, :]
        rows = pl.ds(pl.multiple_of(src_seq * 16, 16), 16)
        cols = pl.ds(pl.multiple_of(dst_seq * 256, 256), 256)
        return q_ref.at[:, cols], qbuf.at[rows, :]

    def kv_copy(part, i):
        dst_seq = lax.rem(seq + i, 16)
        src, dst = piece(part, dst_seq, seq, i)
        return remote(src, dst, kv_send.at[part, i], kv_recv.at[part, i], (req, dst_seq))

    def w_copy(i):
        return remote(
            wt_ref, wbuf.at[m, c], w_send.at[i], w_recv.at[i], (lax.rem(m + i, 16) * 2 + c, seq)
        )

    def start(i, _):
        for part in range(3):
            kv_copy(part, i).start()
        w_copy(i).start()
        return 0

    lax.fori_loop(1, 16, start, 0)
    own = []
    for part in range(3):
        src, dst = piece(part, seq, seq, 0)
        own.append(pltpu.make_async_copy(src, dst, own_sem.at[part]))
    own.append(pltpu.make_async_copy(wt_ref, wbuf.at[m, c], own_sem.at[3]))
    for copy in own:
        copy.start()
    for copy in own:
        copy.wait()

    def kv_wait(i, _):
        for part in range(3):
            kv_copy(part, i).wait()
        return 0

    def w_wait(i, _):
        w_copy(i).wait()
        return 0

    lax.fori_loop(1, 16, w_wait, 0)
    sib = remote(wbuf.at[:, c], wbuf.at[:, c], sib_send, sib_recv, sibling)
    sib.start()
    lax.fori_loop(1, 16, kv_wait, 0)

    length = len_ref[0]
    scale = 1.0 / math.sqrt(HD)
    for head in range(2):

        def tile(i, _):
            rows = pl.ds(pl.multiple_of(i * 64, 64), 64)
            q = qbuf[rows, head * HD : (head + 1) * HD]
            s = lax.dot_general(q, kbuf[...], NT, preferred_element_type=F32) * scale
            col = lax.broadcasted_iota(jnp.int32, (64, D), 1)
            tok = lax.broadcasted_iota(jnp.int32, (64, D), 0) + i * 64
            src, within = col >> 7, col & 127
            behind = jnp.where(
                within < 112, src * 112 + within - length, src * 16 + within - 113 - tok
            )
            seen = behind < 0
            s = jnp.where(seen, s, NEG)
            w = jnp.where(seen, jnp.exp(s - jnp.max(s, axis=-1, keepdims=True)), 0.0)
            total = jnp.sum(w, axis=-1, keepdims=True)
            mixed = jnp.dot(w.astype(BF), vbuf[...], preferred_element_type=F32)
            att[rows, head * HD : (head + 1) * HD] = (mixed / total).astype(BF)
            return 0

        lax.fori_loop(0, 4, tile, 0)

    sib.wait()

    def project(i, _):
        w = wbuf[pl.ds(i * 4, 4)].reshape(512, 256)
        cols = pl.ds(pl.multiple_of(i * 512, 512), 512)
        pbuf[:, cols] = lax.dot_general(att[...], w, NT, preferred_element_type=F32).astype(BF)
        return 0

    lax.fori_loop(0, 4, project, 0)

    def p_copy(i):
        dst_seq = lax.rem(seq + i, 16)
        rows = pl.ds(pl.multiple_of(dst_seq * 16, 16), 16)
        return remote(pbuf.at[rows, :], rbuf.at[i], p_send.at[i], p_recv.at[i], (req, dst_seq))

    def p_start(i, _):
        p_copy(i).start()
        return 0

    def p_wait(i, _):
        p_copy(i).wait()
        return 0

    lax.fori_loop(1, 16, p_start, 0)
    rbuf[0] = pbuf[pl.ds(pl.multiple_of(seq * 16, 16), 16), :]
    lax.fori_loop(1, 16, p_wait, 0)
    projected = lax.fori_loop(
        0, 16, lambda i, acc: acc + rbuf[i].astype(F32), jnp.zeros((16, D), F32)
    )
    residual = (x_ref[...].astype(F32) + projected).astype(BF)
    res_ref[...] = residual
    r = residual.astype(F32)
    mean = jnp.mean(r * r, axis=-1, keepdims=True)
    normed_ref[...] = (r * lax.rsqrt(mean + EPS) * gain_ref[...]).astype(BF)


def attention(cached_len, kv, q, wt, x, gain):
    vm = pl.BlockSpec(memory_space=pltpu.VMEM)
    dma = pltpu.SemaphoreType.DMA
    return pl.pallas_call(
        attention_kernel,
        name="attention",
        out_shape=[jax.ShapeDtypeStruct((16, D), BF)] * 2,
        in_specs=[pl.BlockSpec(memory_space=pltpu.SMEM)] + [vm] * 5,
        out_specs=[vm] * 2,
        scratch_shapes=[
            pltpu.VMEM((2048, HD), BF),
            pltpu.VMEM((2048, HD), BF),
            pltpu.VMEM((256, 256), BF),
            pltpu.VMEM((16, 2, 64, 256), BF),
            pltpu.VMEM((256, 256), BF),
            pltpu.VMEM((256, D), BF),
            pltpu.VMEM((16, 16, D), BF),
            dma((4,)),
            dma((3, 16)), dma((3, 16)),
            dma((16,)), dma((16,)),
            dma, dma,
            dma((16,)), dma((16,)),
        ],
        compiler_params=pltpu.CompilerParams(collective_id=0, has_side_effects=True),
    )(cached_len, kv, q, wt, x, gain)


def experts_kernel(
    normed_ref, res_ref, rt_ref, gt_ref, wg_ref, wd_ref, out_ref,
    tok, comb, xs, xr, po, pr, sl, rl, sr, rr, fs, fr,
    z_send, z_recv, y_send, y_recv, x_send, x_recv, b_send, b_recv, r_send, r_recv, f_send, f_recv,
):
    x, y, z, c = coords()
    q = x * 2 + c
    right, left = device(x, lax.rem(y + 1, 8), z, c), device(x, lax.rem(y + 7, 8), z, c)

    def at_q(j):
        n = lax.rem(q + j, 8)
        return device(n // 2, y, z, lax.rem(n, 2))

    zs = [device(x, y, lax.rem(z + i, 8), c) for i in range(1, 8)]
    greet(zs + [right, left] + [at_q(j) for j in range(1, 8)])

    own_rows = pl.ds(pl.multiple_of(z * 16, 16), 16)

    def z_copy(i):
        dev = device(x, y, lax.rem(z + i, 8), c)
        return remote(normed_ref, tok.at[0, own_rows], z_send.at[i], z_recv.at[i], dev)

    for i in range(1, 8):
        z_copy(i).start()
    tok[0, own_rows] = normed_ref[...]
    for i in range(1, 8):
        z_copy(i).wait()

    def half(h):
        return pl.ds(h * 1024, 1024)

    def y_copy(way, t, h):
        if way == 0:
            a, b, dev = t, t + 1, right
        else:
            a, b, dev = (8 - t) % 8, 7 - t, left
        return remote(
            tok.at[a, :, half(h)], tok.at[b, :, half(h)], y_send.at[way, t, h], y_recv.at[way, t, h], dev
        )

    def steps(t):
        return [(0, 0), (1, 0), (0, 1), (1, 1)] if t < 3 else [(0, 0), (1, 1)]

    def x_copy(o, j):
        return remote(xs.at[o, j], xr.at[o, j], x_send.at[o, j], x_recv.at[o, j], at_q(j))

    def b_copy(o, j):
        return remote(po.at[o, j], pr.at[o, j], b_send.at[o, j], b_recv.at[o, j], at_q(8 - j))

    seq, zhi = (z % 2) * 8 + y, z // 2

    def select(o):
        y0 = lax.rem(y + 8 - o, 8)
        rt, gt = rt_ref[y0], gt_ref[y0]
        row = lax.broadcasted_iota(jnp.int32, (128, 128), 0)
        col = lax.broadcasted_iota(jnp.int32, (128, 128), 1)
        expert = 4 * (zhi * 8 + ((q + (row >> 4)) & 7)) + seq // 4
        same = ((row >> 1) & 7) == (col >> 4)
        match = jnp.zeros((128, 128), F32)
        gate = jnp.zeros((128, 128), F32)
        for k in range(8):
            hit = same & (rt[k : k + 1, :] == expert)
            match = jnp.where(hit, 1.0, match)
            gate = jnp.where(hit, gt[k : k + 1, :], gate)
        before = jnp.where(row < col, 1.0, 0.0).astype(BF)
        rank = jnp.dot(match.astype(BF), before, preferred_element_type=F32)
        pick = jnp.where(rank == (row & 1).astype(F32), match, 0.0)
        comb[o] = (pick * gate).T.astype(BF)
        pick = pick.astype(BF)

        def tile(n, _):
            cols = pl.ds(pl.multiple_of(n * 512, 512), 512)
            rows = jnp.dot(pick, tok[o, :, cols], preferred_element_type=F32).astype(BF)
            xs[o, :, :, cols] = rows.reshape(8, 16, 512)
            xr[o, 0, :, cols] = rows[:16]
            return 0

        lax.fori_loop(0, 4, tile, 0)

        def send(j, _):
            x_copy(o, j).start()
            return 0

        lax.fori_loop(1, 8, send, 0)

    def feed(o):
        def arrive(j, _):
            x_copy(o, j).wait_recv()
            return 0

        lax.fori_loop(1, 8, arrive, 0)
        both = jnp.dot(xr[o].reshape(128, D), wg_ref[...], preferred_element_type=F32)
        g, u = both[:, :192], both[:, 192:]
        hidden = (g / (1.0 + jnp.exp(-g)) * u).astype(BF)

        def tile(n, _):
            cols = pl.ds(pl.multiple_of(n * 512, 512), 512)
            rows = jnp.dot(hidden, wd_ref[:, cols], preferred_element_type=F32).astype(BF)
            po[o, :, :, cols] = rows.reshape(8, 16, 512)
            pr[o, 0, :, cols] = rows[:16]
            return 0

        lax.fori_loop(0, 4, tile, 0)

        def send(j, _):
            b_copy(o, j).start()
            return 0

        lax.fori_loop(1, 8, send, 0)

    def returned(o):
        def arrive(j, _):
            b_copy(o, j).wait_recv()
            return 0

        lax.fori_loop(1, 8, arrive, 0)

    def combined(o, cols):
        rows = pr[o, :, :, cols].reshape(128, cols.size)
        return jnp.dot(comb[o], rows, preferred_element_type=F32)

    def pair(f, o):
        def one(i, _):
            f(jnp.where(i == 0, o, 8 - o))
            return 0

        lax.fori_loop(0, 2, one, 0)

    for way, h in steps(0):
        y_copy(way, 0, h).start()
    select(0)
    for t in range(1, 4):
        for way, h in steps(t - 1):
            y_copy(way, t - 1, h).wait_recv()
            if (way, h) in steps(t):
                y_copy(way, t, h).start()
        pair(select, t)
        if t == 1:
            feed(0)
        else:
            pair(feed, t - 1)
    for way, h in steps(3):
        y_copy(way, 3, h).wait_recv()
    select(4)
    pair(feed, 3)
    feed(4)

    def r_copy(way, t, h):
        src, dst, dev = (sl, rl, left) if way == 0 else (sr, rr, right)
        return remote(
            src.at[t, :, half(h)], dst.at[t, :, half(h)], r_send.at[way, t, h], r_recv.at[way, t, h], dev
        )

    def r_steps(t):
        return [(0, 0), (1, 1)] if t == 0 else [(0, 0), (1, 1), (0, 1), (1, 0)]

    for t in range(4):
        for o in {4 - t, 4 + t}:
            returned(o)
        for way, h in r_steps(t):
            o = 4 - t if way == 0 else 4 + t
            came = t > 0 and (way, h) in r_steps(t - 1)
            if came:
                r_copy(way, t - 1, h).wait_recv()
            src, dst = (sl, rl) if way == 0 else (sr, rr)

            def tile(n, _):
                cols = pl.ds(pl.multiple_of(h * 1024 + n * 512, 512), 512)
                part = combined(o, cols)
                if came:
                    part = part + dst[t - 1, :, cols].astype(F32)
                src[t, :, cols] = part.astype(BF)
                return 0

            lax.fori_loop(0, 2, tile, 0)
            r_copy(way, t, h).start()

    returned(0)
    for way, h in r_steps(3):
        r_copy(way, 3, h).wait_recv()

    def total(n, _):
        cols = pl.ds(pl.multiple_of(n * 512, 512), 512)
        part = combined(0, cols) + rl[3, :, cols].astype(F32) + rr[3, :, cols].astype(F32)
        fs[:, cols] = part.astype(BF)
        return 0

    lax.fori_loop(0, 4, total, 0)

    def f_copy(i):
        n = lax.rem(z + i, 8)
        rows = pl.ds(pl.multiple_of(n * 16, 16), 16)
        return remote(fs.at[rows, :], fr.at[i], f_send.at[i], f_recv.at[i], device(x, y, n, c))

    for i in range(1, 8):
        f_copy(i).start()
    acc = res_ref[...].astype(F32) + fs[own_rows, :].astype(F32)
    for i in range(1, 8):
        f_copy(i).wait()
        acc = acc + fr[i].astype(F32)
    out_ref[...] = acc.astype(BF)

    for t in range(4):
        for way, h in steps(t):
            y_copy(way, t, h).wait_send()
        for way, h in r_steps(t):
            r_copy(way, t, h).wait_send()

    def sent(o, _):
        def one(j, _):
            x_copy(o, j).wait_send()
            b_copy(o, j).wait_send()
            return 0

        return lax.fori_loop(1, 8, one, 0)

    lax.fori_loop(0, 8, sent, 0)


def experts(normed, residual, rt, gt, wg, wd):
    vm = pl.BlockSpec(memory_space=pltpu.VMEM)
    dma = pltpu.SemaphoreType.DMA
    big = pltpu.VMEM((8, 8, 16, D), BF)
    hop = pltpu.VMEM((4, 128, D), BF)
    return pl.pallas_call(
        experts_kernel,
        name="experts",
        out_shape=jax.ShapeDtypeStruct((16, D), BF),
        in_specs=[vm] * 6,
        out_specs=vm,
        scratch_shapes=[
            pltpu.VMEM((8, 128, D), BF),
            pltpu.VMEM((8, 128, 128), BF),
            big, big, big, big,
            hop, hop, hop, hop,
            pltpu.VMEM((128, D), BF),
            pltpu.VMEM((8, 16, D), BF),
            dma((8,)), dma((8,)),
            dma((2, 4, 2)), dma((2, 4, 2)),
            dma((8, 8)), dma((8, 8)),
            dma((8, 8)), dma((8, 8)),
            dma((2, 4, 2)), dma((2, 4, 2)),
            dma((8,)), dma((8,)),
        ],
        compiler_params=pltpu.CompilerParams(
            collective_id=1, has_side_effects=True, vmem_limit_bytes=56 * 1024 * 1024
        ),
    )(normed, residual, rt, gt, wg, wd)


def local(
    layer_input, queries, fresh_kv, cache_kv, cached_len, out_weight, norm_gain,
    routes, route_gates, w_gate_up, w_down,
):
    x, y, z, c = coords()

    def table(a):
        whole = lax.all_gather(a[0].T.reshape(1, 128), ("req", "seq"), axis=0, tiled=True)
        whole = whole.reshape(4, 8, 2, 8, 128)
        mine = lax.dynamic_slice_in_dim(whole, x * 2 + c, 1, axis=1)[:, 0]
        return mine.reshape(4, 2, 8, 8, 16).transpose(2, 3, 0, 1, 4).reshape(8, 8, 128)

    rt, gt = table(routes), table(route_gates)
    kv = jnp.concatenate([cache_kv[0], fresh_kv[0]], 0)
    residual, normed = attention(
        cached_len, kv, queries[0], out_weight.T, layer_input[0], norm_gain[None]
    )
    return experts(normed, residual, rt, gt, w_gate_up[0], w_down[0])[None]


def solution(mesh):
    return jax.shard_map(
        local,
        mesh=mesh,
        in_specs=(
            P("req", "seq", None),
            P("req", "seq", None),
            P("req", "seq", None),
            P("req", "seq", None),
            P("req"),
            P("seq", "req"),
            P(),
            P("req", "seq", None),
            P("req", "seq", None),
            P(("req", "seq"), None, None),
            P(("req", "seq"), None, None),
        ),
        out_specs=P("req", "seq", None),
        check_vma=False,
    )
```

```python
import math

import jax
import jax.numpy as jnp
from jax import lax
from jax.experimental import pallas as pl
from jax.experimental.pallas import tpu as pltpu
from jax.sharding import PartitionSpec as P

MESH = pl.DeviceIdType.MESH
BF = jnp.bfloat16
F32 = jnp.float32
NEG = -1e30
EPS = 1e-06
D = 2048
HD = 128
NT = (((1,), (1,)), ((), ()))


def coords():
    req, seq = lax.axis_index("req"), lax.axis_index("seq")
    z = (req // 8) * 2 + seq // 8
    return (req // 2) % 4, seq % 8, z, req % 2


def device(x, y, z, c):
    return ((z // 2) * 8 + x * 2 + c, (z % 2) * 8 + y)


def remote(src, dst, send, recv, dev):
    return pltpu.make_async_remote_copy(
        src_ref=src, dst_ref=dst, send_sem=send, recv_sem=recv, device_id=dev, device_id_type=MESH
    )


def greet(devs):
    barrier = pltpu.get_barrier_semaphore()
    for dev in devs:
        pl.semaphore_signal(barrier, inc=1, device_id=dev, device_id_type=MESH)
    pl.semaphore_wait(barrier, len(devs))


def attention_kernel(
    len_ref, kv_ref, q_ref, wt_ref, x_ref, gain_ref, mark_ref, res_ref, normed_ref, table_ref,
    marks, near, far, kbuf, vbuf, qbuf, wbuf, att, pbuf, rbuf,
    m_send, m_recv, n_send, n_recv, own_sem, kv_send, kv_recv, w_send, w_recv, sib_send, sib_recv, p_send, p_recv,
):
    req, seq = lax.axis_index("req"), lax.axis_index("seq")
    m, c = req // 2, req % 2
    peers = [(req, lax.rem(seq + i, 16)) for i in range(1, 16)]
    chips = [(lax.rem(m + i, 16) * 2 + c, seq) for i in range(1, 16)]
    sibling = (m * 2 + 1 - c, seq)
    greet(peers + chips + [sibling])

    def piece(part, dst_seq, src_seq, i):
        rows = pl.ds(pl.multiple_of(src_seq * 128, 128), 128)
        head = dst_seq // 4
        if part == 0:
            cols = pl.ds(pl.multiple_of(head * HD, HD), HD)
            return kv_ref.at[:, cols], kbuf.at[rows, :]
        if part == 1:
            cols = pl.ds(pl.multiple_of(512 + head * HD, HD), HD)
            return kv_ref.at[:, cols], vbuf.at[rows, :]
        rows = pl.ds(pl.multiple_of(src_seq * 16, 16), 16)
        cols = pl.ds(pl.multiple_of(dst_seq * 256, 256), 256)
        return q_ref.at[:, cols], qbuf.at[rows, :]

    def kv_copy(part, i):
        dst_seq = lax.rem(seq + i, 16)
        src, dst = piece(part, dst_seq, seq, i)
        return remote(src, dst, kv_send.at[part, i], kv_recv.at[part, i], (req, dst_seq))

    def w_copy(i):
        return remote(
            wt_ref, wbuf.at[m, c], w_send.at[i], w_recv.at[i], (lax.rem(m + i, 16) * 2 + c, seq)
        )

    def mark_copy(i):
        dst_seq = lax.rem(seq + i, 16)
        return remote(mark_ref, marks.at[seq], m_send.at[i], m_recv.at[i], (req, dst_seq))

    def near_copy(i):
        dst = (lax.rem(req + 8 * i, 32), seq)
        return remote(near, far.at[i], n_send.at[i], n_recv.at[i], dst)

    def mark_wait(i, _):
        mark_copy(i).wait()
        return 0

    def start(i, _):
        mark_copy(i).start()
        for part in range(3):
            kv_copy(part, i).start()
        w_copy(i).start()
        return 0

    lax.fori_loop(1, 16, start, 0)
    own = []
    for part in range(3):
        src, dst = piece(part, seq, seq, 0)
        own.append(pltpu.make_async_copy(src, dst, own_sem.at[part]))
    own.append(pltpu.make_async_copy(wt_ref, wbuf.at[m, c], own_sem.at[3]))
    own.append(pltpu.make_async_copy(mark_ref, marks.at[seq], own_sem.at[4]))
    for copy in own:
        copy.start()
    for copy in own:
        copy.wait()

    def kv_wait(i, _):
        for part in range(3):
            kv_copy(part, i).wait()
        return 0

    def w_wait(i, _):
        w_copy(i).wait()
        return 0

    lax.fori_loop(1, 16, mark_wait, 0)
    for n in range(8):
        near[n] = marks[n] + marks[8 + n]
    for i in range(1, 4):
        near_copy(i).start()
    lax.fori_loop(1, 16, w_wait, 0)
    sib = remote(wbuf.at[:, c], wbuf.at[:, c], sib_send, sib_recv, sibling)
    sib.start()
    lax.fori_loop(1, 16, kv_wait, 0)

    length = len_ref[0]
    scale = 1.0 / math.sqrt(HD)
    for head in range(2):

        def tile(i, _):
            rows = pl.ds(pl.multiple_of(i * 64, 64), 64)
            q = qbuf[rows, head * HD : (head + 1) * HD]
            s = lax.dot_general(q, kbuf[...], NT, preferred_element_type=F32) * scale
            col = lax.broadcasted_iota(jnp.int32, (64, D), 1)
            tok = lax.broadcasted_iota(jnp.int32, (64, D), 0) + i * 64
            src, within = col >> 7, col & 127
            behind = jnp.where(
                within < 112, src * 112 + within - length, src * 16 + within - 113 - tok
            )
            seen = behind < 0
            s = jnp.where(seen, s, NEG)
            w = jnp.where(seen, jnp.exp(s - jnp.max(s, axis=-1, keepdims=True)), 0.0)
            total = jnp.sum(w, axis=-1, keepdims=True)
            mixed = jnp.dot(w.astype(BF), vbuf[...], preferred_element_type=F32)
            att[rows, head * HD : (head + 1) * HD] = (mixed / total).astype(BF)
            return 0

        lax.fori_loop(0, 4, tile, 0)

    sib.wait()

    def project(i, _):
        w = wbuf[pl.ds(i * 4, 4)].reshape(512, 256)
        cols = pl.ds(pl.multiple_of(i * 512, 512), 512)
        pbuf[:, cols] = lax.dot_general(att[...], w, NT, preferred_element_type=F32).astype(BF)
        return 0

    lax.fori_loop(0, 4, project, 0)

    def p_copy(i):
        dst_seq = lax.rem(seq + i, 16)
        rows = pl.ds(pl.multiple_of(dst_seq * 16, 16), 16)
        return remote(pbuf.at[rows, :], rbuf.at[i], p_send.at[i], p_recv.at[i], (req, dst_seq))

    def p_start(i, _):
        p_copy(i).start()
        return 0

    def p_wait(i, _):
        p_copy(i).wait()
        return 0

    lax.fori_loop(1, 16, p_start, 0)
    for i in range(1, 4):
        near_copy(i).wait()
    for n in range(8):
        table_ref[n] = near[n] + far[1, n] + far[2, n] + far[3, n]
    rbuf[0] = pbuf[pl.ds(pl.multiple_of(seq * 16, 16), 16), :]
    lax.fori_loop(1, 16, p_wait, 0)
    projected = lax.fori_loop(
        0, 16, lambda i, acc: acc + rbuf[i].astype(F32), jnp.zeros((16, D), F32)
    )
    residual = (x_ref[...].astype(F32) + projected).astype(BF)
    res_ref[...] = residual
    r = residual.astype(F32)
    mean = jnp.mean(r * r, axis=-1, keepdims=True)
    normed_ref[...] = (r * lax.rsqrt(mean + EPS) * gain_ref[...]).astype(BF)


def attention(cached_len, kv, q, wt, x, gain, mark):
    vm = pl.BlockSpec(memory_space=pltpu.VMEM)
    dma = pltpu.SemaphoreType.DMA
    return pl.pallas_call(
        attention_kernel,
        name="attention",
        out_shape=[jax.ShapeDtypeStruct((16, D), BF)] * 2
        + [jax.ShapeDtypeStruct((8, 16, 128), F32)],
        in_specs=[pl.BlockSpec(memory_space=pltpu.SMEM)] + [vm] * 6,
        out_specs=[vm] * 3,
        scratch_shapes=[
            pltpu.VMEM((16, 16, 128), F32),
            pltpu.VMEM((8, 16, 128), F32),
            pltpu.VMEM((4, 8, 16, 128), F32),
            pltpu.VMEM((2048, HD), BF),
            pltpu.VMEM((2048, HD), BF),
            pltpu.VMEM((256, 256), BF),
            pltpu.VMEM((16, 2, 64, 256), BF),
            pltpu.VMEM((256, 256), BF),
            pltpu.VMEM((256, D), BF),
            pltpu.VMEM((16, 16, D), BF),
            dma((16,)), dma((16,)),
            dma((4,)), dma((4,)),
            dma((5,)),
            dma((3, 16)), dma((3, 16)),
            dma((16,)), dma((16,)),
            dma, dma,
            dma((16,)), dma((16,)),
        ],
        compiler_params=pltpu.CompilerParams(collective_id=0, has_side_effects=True),
    )(cached_len, kv, q, wt, x, gain, mark)


def experts_kernel(
    normed_ref, res_ref, table_ref, wg_ref, wd_ref, out_ref,
    tok, comb, xs, xr, po, pr, sl, rl, sr, rr, fs, fr,
    z_send, z_recv, y_send, y_recv, x_send, x_recv, b_send, b_recv, r_send, r_recv, f_send, f_recv,
):
    x, y, z, c = coords()
    q = x * 2 + c
    right, left = device(x, lax.rem(y + 1, 8), z, c), device(x, lax.rem(y + 7, 8), z, c)

    def at_q(j):
        n = lax.rem(q + j, 8)
        return device(n // 2, y, z, lax.rem(n, 2))

    zs = [device(x, y, lax.rem(z + i, 8), c) for i in range(1, 8)]
    greet(zs + [right, left] + [at_q(j) for j in range(1, 8)])

    own_rows = pl.ds(pl.multiple_of(z * 16, 16), 16)

    def z_copy(i):
        dev = device(x, y, lax.rem(z + i, 8), c)
        return remote(normed_ref, tok.at[0, own_rows], z_send.at[i], z_recv.at[i], dev)

    for i in range(1, 8):
        z_copy(i).start()
    tok[0, own_rows] = normed_ref[...]
    for i in range(1, 8):
        z_copy(i).wait()

    def half(h):
        return pl.ds(h * 1024, 1024)

    def y_copy(way, t, h):
        if way == 0:
            a, b, dev = t, t + 1, right
        else:
            a, b, dev = (8 - t) % 8, 7 - t, left
        return remote(
            tok.at[a, :, half(h)], tok.at[b, :, half(h)], y_send.at[way, t, h], y_recv.at[way, t, h], dev
        )

    def steps(t):
        return [(0, 0), (1, 0), (0, 1), (1, 1)] if t < 3 else [(0, 0), (1, 1)]

    def x_copy(o, j):
        return remote(xs.at[o, j], xr.at[o, j], x_send.at[o, j], x_recv.at[o, j], at_q(j))

    def b_copy(o, j):
        return remote(po.at[o, j], pr.at[o, j], b_send.at[o, j], b_recv.at[o, j], at_q(8 - j))

    seq, zhi = (z % 2) * 8 + y, z // 2

    def select(o):
        y0 = lax.rem(y + 8 - o, 8)
        table = table_ref[y0]
        row = lax.broadcasted_iota(jnp.int32, (128, 128), 0)
        col = lax.broadcasted_iota(jnp.int32, (128, 128), 1)
        expert = (4 * (zhi * 8 + ((q + (row >> 4)) & 7)) + seq // 4).astype(F32)
        same = ((row >> 1) & 7) == (col >> 4)
        match = jnp.zeros((128, 128), F32)
        gate = jnp.zeros((128, 128), F32)
        for k in range(8):
            hit = same & (table[k : k + 1, :] == expert)
            match = jnp.where(hit, 1.0, match)
            gate = jnp.where(hit, table[8 + k : 9 + k, :], gate)
        before = jnp.where(row < col, 1.0, 0.0).astype(BF)
        rank = jnp.dot(match.astype(BF), before, preferred_element_type=F32)
        pick = jnp.where(rank == (row & 1).astype(F32), match, 0.0)
        comb[o] = (pick * gate).T.astype(BF)
        pick = pick.astype(BF)

        def tile(n, _):
            cols = pl.ds(pl.multiple_of(n * 512, 512), 512)
            rows = jnp.dot(pick, tok[o, :, cols], preferred_element_type=F32).astype(BF)
            xs[o, :, :, cols] = rows.reshape(8, 16, 512)
            xr[o, 0, :, cols] = rows[:16]
            return 0

        lax.fori_loop(0, 4, tile, 0)

        def send(j, _):
            x_copy(o, j).start()
            return 0

        lax.fori_loop(1, 8, send, 0)

    def feed(o):
        def arrive(j, _):
            x_copy(o, j).wait_recv()
            return 0

        lax.fori_loop(1, 8, arrive, 0)
        both = jnp.dot(xr[o].reshape(128, D), wg_ref[...], preferred_element_type=F32)
        g, u = both[:, :192], both[:, 192:]
        hidden = (g / (1.0 + jnp.exp(-g)) * u).astype(BF)

        def tile(n, _):
            cols = pl.ds(pl.multiple_of(n * 512, 512), 512)
            rows = jnp.dot(hidden, wd_ref[:, cols], preferred_element_type=F32).astype(BF)
            po[o, :, :, cols] = rows.reshape(8, 16, 512)
            pr[o, 0, :, cols] = rows[:16]
            return 0

        lax.fori_loop(0, 4, tile, 0)

        def send(j, _):
            b_copy(o, j).start()
            return 0

        lax.fori_loop(1, 8, send, 0)

    def returned(o):
        def arrive(j, _):
            b_copy(o, j).wait_recv()
            return 0

        lax.fori_loop(1, 8, arrive, 0)

    def combined(o, cols):
        rows = pr[o, :, :, cols].reshape(128, cols.size)
        return jnp.dot(comb[o], rows, preferred_element_type=F32)

    def pair(f, o):
        def one(i, _):
            f(jnp.where(i == 0, o, 8 - o))
            return 0

        lax.fori_loop(0, 2, one, 0)

    for way, h in steps(0):
        y_copy(way, 0, h).start()
    select(0)
    for t in range(1, 4):
        for way, h in steps(t - 1):
            y_copy(way, t - 1, h).wait_recv()
            if (way, h) in steps(t):
                y_copy(way, t, h).start()
        pair(select, t)
        if t == 1:
            feed(0)
        else:
            pair(feed, t - 1)
    for way, h in steps(3):
        y_copy(way, 3, h).wait_recv()
    select(4)
    pair(feed, 3)
    feed(4)

    def r_copy(way, t, h):
        src, dst, dev = (sl, rl, left) if way == 0 else (sr, rr, right)
        return remote(
            src.at[t, :, half(h)], dst.at[t, :, half(h)], r_send.at[way, t, h], r_recv.at[way, t, h], dev
        )

    def r_steps(t):
        return [(0, 0), (1, 1)] if t == 0 else [(0, 0), (1, 1), (0, 1), (1, 0)]

    for t in range(4):
        for o in {4 - t, 4 + t}:
            returned(o)
        for way, h in r_steps(t):
            o = 4 - t if way == 0 else 4 + t
            came = t > 0 and (way, h) in r_steps(t - 1)
            if came:
                r_copy(way, t - 1, h).wait_recv()
            src, dst = (sl, rl) if way == 0 else (sr, rr)

            def tile(n, _):
                cols = pl.ds(pl.multiple_of(h * 1024 + n * 512, 512), 512)
                part = combined(o, cols)
                if came:
                    part = part + dst[t - 1, :, cols].astype(F32)
                src[t, :, cols] = part.astype(BF)
                return 0

            lax.fori_loop(0, 2, tile, 0)
            r_copy(way, t, h).start()

    returned(0)
    for way, h in r_steps(3):
        r_copy(way, 3, h).wait_recv()

    def total(n, _):
        cols = pl.ds(pl.multiple_of(n * 512, 512), 512)
        part = combined(0, cols) + rl[3, :, cols].astype(F32) + rr[3, :, cols].astype(F32)
        fs[:, cols] = part.astype(BF)
        return 0

    lax.fori_loop(0, 4, total, 0)

    def f_copy(i):
        n = lax.rem(z + i, 8)
        rows = pl.ds(pl.multiple_of(n * 16, 16), 16)
        return remote(fs.at[rows, :], fr.at[i], f_send.at[i], f_recv.at[i], device(x, y, n, c))

    for i in range(1, 8):
        f_copy(i).start()
    acc = res_ref[...].astype(F32) + fs[own_rows, :].astype(F32)
    for i in range(1, 8):
        f_copy(i).wait()
        acc = acc + fr[i].astype(F32)
    out_ref[...] = acc.astype(BF)

    for t in range(4):
        for way, h in steps(t):
            y_copy(way, t, h).wait_send()
        for way, h in r_steps(t):
            r_copy(way, t, h).wait_send()

    def sent(o, _):
        def one(j, _):
            x_copy(o, j).wait_send()
            b_copy(o, j).wait_send()
            return 0

        return lax.fori_loop(1, 8, one, 0)

    lax.fori_loop(0, 8, sent, 0)


def experts(normed, residual, table, wg, wd):
    vm = pl.BlockSpec(memory_space=pltpu.VMEM)
    dma = pltpu.SemaphoreType.DMA
    big = pltpu.VMEM((8, 8, 16, D), BF)
    hop = pltpu.VMEM((4, 128, D), BF)
    return pl.pallas_call(
        experts_kernel,
        name="experts",
        out_shape=jax.ShapeDtypeStruct((16, D), BF),
        in_specs=[vm] * 5,
        out_specs=vm,
        scratch_shapes=[
            pltpu.VMEM((8, 128, D), BF),
            pltpu.VMEM((8, 128, 128), BF),
            big, big, big, big,
            hop, hop, hop, hop,
            pltpu.VMEM((128, D), BF),
            pltpu.VMEM((8, 16, D), BF),
            dma((8,)), dma((8,)),
            dma((2, 4, 2)), dma((2, 4, 2)),
            dma((8, 8)), dma((8, 8)),
            dma((8, 8)), dma((8, 8)),
            dma((2, 4, 2)), dma((2, 4, 2)),
            dma((8,)), dma((8,)),
        ],
        compiler_params=pltpu.CompilerParams(
            collective_id=1, has_side_effects=True, vmem_limit_bytes=56 * 1024 * 1024
        ),
    )(normed, residual, table, wg, wd)


def local(
    layer_input, queries, fresh_kv, cache_kv, cached_len, out_weight, norm_gain,
    routes, route_gates, w_gate_up, w_down,
):
    z = coords()[2]
    mark = jnp.concatenate([routes[0].T.astype(F32), route_gates[0].T], 0)
    mark = jnp.where(jnp.arange(128)[None] // 16 == z, jnp.tile(mark, (1, 8)), 0.0)
    kv = jnp.concatenate([cache_kv[0], fresh_kv[0]], 0)
    residual, normed, table = attention(
        cached_len, kv, queries[0], out_weight.T, layer_input[0], norm_gain[None], mark
    )
    return experts(normed, residual, table, w_gate_up[0], w_down[0])[None]


def solution(mesh):
    return jax.shard_map(
        local,
        mesh=mesh,
        in_specs=(
            P("req", "seq", None),
            P("req", "seq", None),
            P("req", "seq", None),
            P("req", "seq", None),
            P("req"),
            P("seq", "req"),
            P(),
            P("req", "seq", None),
            P("req", "seq", None),
            P(("req", "seq"), None, None),
            P(("req", "seq"), None, None),
        ),
        out_specs=P("req", "seq", None),
        check_vma=False,
    )
```

```python
import math

import jax
import jax.numpy as jnp
from jax import lax
from jax.experimental import pallas as pl
from jax.experimental.pallas import tpu as pltpu
from jax.sharding import PartitionSpec as P

MESH = pl.DeviceIdType.MESH
BF = jnp.bfloat16
F32 = jnp.float32
NEG = -1e30
EPS = 1e-06
D = 2048
HD = 128
NT = (((1,), (1,)), ((), ()))


def coords():
    req, seq = lax.axis_index("req"), lax.axis_index("seq")
    z = (req // 8) * 2 + seq // 8
    return (req // 2) % 4, seq % 8, z, req % 2


def device(x, y, z, c):
    return ((z // 2) * 8 + x * 2 + c, (z % 2) * 8 + y)


def remote(src, dst, send, recv, dev):
    return pltpu.make_async_remote_copy(
        src_ref=src, dst_ref=dst, send_sem=send, recv_sem=recv, device_id=dev, device_id_type=MESH
    )


def greet(devs):
    barrier = pltpu.get_barrier_semaphore()
    for dev in devs:
        pl.semaphore_signal(barrier, inc=1, device_id=dev, device_id_type=MESH)
    pl.semaphore_wait(barrier, len(devs))


def attention_kernel(
    len_ref, kv_ref, q_ref, wt_ref, x_ref, gain_ref, mark_ref, res_ref, normed_ref, table_ref,
    marks, near, far, kbuf, vbuf, qbuf, wbuf, att, pbuf, rbuf,
    m_send, m_recv, n_send, n_recv, own_sem, kv_send, kv_recv, w_send, w_recv, sib_send, sib_recv, p_send, p_recv,
):
    req, seq = lax.axis_index("req"), lax.axis_index("seq")
    m, c = req // 2, req % 2
    peers = [(req, lax.rem(seq + i, 16)) for i in range(1, 16)]
    chips = [(lax.rem(m + i, 16) * 2 + c, seq) for i in range(1, 16)]
    sibling = (m * 2 + 1 - c, seq)
    greet(peers + chips + [sibling])

    def piece(part, dst_seq, src_seq, i):
        rows = pl.ds(pl.multiple_of(src_seq * 128, 128), 128)
        head = dst_seq // 4
        if part == 0:
            cols = pl.ds(pl.multiple_of(head * HD, HD), HD)
            return kv_ref.at[:, cols], kbuf.at[rows, :]
        if part == 1:
            cols = pl.ds(pl.multiple_of(512 + head * HD, HD), HD)
            return kv_ref.at[:, cols], vbuf.at[rows, :]
        rows = pl.ds(pl.multiple_of(src_seq * 16, 16), 16)
        cols = pl.ds(pl.multiple_of(dst_seq * 256, 256), 256)
        return q_ref.at[:, cols], qbuf.at[rows, :]

    def kv_copy(part, i):
        dst_seq = lax.rem(seq + i, 16)
        src, dst = piece(part, dst_seq, seq, i)
        return remote(src, dst, kv_send.at[part, i], kv_recv.at[part, i], (req, dst_seq))

    def w_copy(i):
        return remote(
            wt_ref, wbuf.at[m, c], w_send.at[i], w_recv.at[i], (lax.rem(m + i, 16) * 2 + c, seq)
        )

    def mark_copy(i):
        dst_seq = lax.rem(seq + i, 16)
        return remote(mark_ref, marks.at[seq], m_send.at[i], m_recv.at[i], (req, dst_seq))

    def near_copy(i):
        dst = (lax.rem(req + 8 * i, 32), seq)
        return remote(near, far.at[i], n_send.at[i], n_recv.at[i], dst)

    def mark_wait(i, _):
        mark_copy(i).wait()
        return 0

    def start(i, _):
        mark_copy(i).start()
        for part in range(3):
            kv_copy(part, i).start()
        w_copy(i).start()
        return 0

    lax.fori_loop(1, 16, start, 0)
    own = []
    for part in range(3):
        src, dst = piece(part, seq, seq, 0)
        own.append(pltpu.make_async_copy(src, dst, own_sem.at[part]))
    own.append(pltpu.make_async_copy(wt_ref, wbuf.at[m, c], own_sem.at[3]))
    own.append(pltpu.make_async_copy(mark_ref, marks.at[seq], own_sem.at[4]))
    for copy in own:
        copy.start()
    for copy in own:
        copy.wait()

    def kv_wait(i, _):
        for part in range(3):
            kv_copy(part, i).wait()
        return 0

    def w_wait(i, _):
        w_copy(i).wait()
        return 0

    lax.fori_loop(1, 16, mark_wait, 0)
    for n in range(8):
        near[n] = marks[n] + marks[8 + n]
    for i in range(1, 4):
        near_copy(i).start()
    lax.fori_loop(1, 16, w_wait, 0)
    sib = remote(wbuf.at[:, c], wbuf.at[:, c], sib_send, sib_recv, sibling)
    sib.start()
    lax.fori_loop(1, 16, kv_wait, 0)

    length = len_ref[0]
    scale = 1.0 / math.sqrt(HD)
    for head in range(2):

        def tile(i, _):
            rows = pl.ds(pl.multiple_of(i * 64, 64), 64)
            q = qbuf[rows, head * HD : (head + 1) * HD]
            s = lax.dot_general(q, kbuf[...], NT, preferred_element_type=F32) * scale
            col = lax.broadcasted_iota(jnp.int32, (64, D), 1)
            tok = lax.broadcasted_iota(jnp.int32, (64, D), 0) + i * 64
            src, within = col >> 7, col & 127
            behind = jnp.where(
                within < 112, src * 112 + within - length, src * 16 + within - 113 - tok
            )
            seen = behind < 0
            s = jnp.where(seen, s, NEG)
            w = jnp.where(seen, jnp.exp(s - jnp.max(s, axis=-1, keepdims=True)), 0.0)
            total = jnp.sum(w, axis=-1, keepdims=True)
            mixed = jnp.dot(w.astype(BF), vbuf[...], preferred_element_type=F32)
            att[rows, head * HD : (head + 1) * HD] = (mixed / total).astype(BF)
            return 0

        lax.fori_loop(0, 4, tile, 0)

    sib.wait()

    def project(i, _):
        w = wbuf[pl.ds(i * 4, 4)].reshape(512, 256)
        cols = pl.ds(pl.multiple_of(i * 512, 512), 512)
        pbuf[:, cols] = lax.dot_general(att[...], w, NT, preferred_element_type=F32).astype(BF)
        return 0

    lax.fori_loop(0, 4, project, 0)

    def p_copy(i):
        dst_seq = lax.rem(seq + i, 16)
        rows = pl.ds(pl.multiple_of(dst_seq * 16, 16), 16)
        return remote(pbuf.at[rows, :], rbuf.at[i], p_send.at[i], p_recv.at[i], (req, dst_seq))

    def p_start(i, _):
        p_copy(i).start()
        return 0

    def p_wait(i, _):
        p_copy(i).wait()
        return 0

    lax.fori_loop(1, 16, p_start, 0)
    for i in range(1, 4):
        near_copy(i).wait()
    for n in range(8):
        table_ref[n] = near[n] + far[1, n] + far[2, n] + far[3, n]
    rbuf[0] = pbuf[pl.ds(pl.multiple_of(seq * 16, 16), 16), :]
    lax.fori_loop(1, 16, p_wait, 0)
    projected = lax.fori_loop(
        0, 16, lambda i, acc: acc + rbuf[i].astype(F32), jnp.zeros((16, D), F32)
    )
    residual = (x_ref[...].astype(F32) + projected).astype(BF)
    res_ref[...] = residual
    r = residual.astype(F32)
    mean = jnp.mean(r * r, axis=-1, keepdims=True)
    normed_ref[...] = (r * lax.rsqrt(mean + EPS) * gain_ref[...]).astype(BF)


def attention(cached_len, kv, q, wt, x, gain, mark):
    vm = pl.BlockSpec(memory_space=pltpu.VMEM)
    dma = pltpu.SemaphoreType.DMA
    return pl.pallas_call(
        attention_kernel,
        name="attention",
        out_shape=[jax.ShapeDtypeStruct((16, D), BF)] * 2
        + [jax.ShapeDtypeStruct((8, 16, 128), F32)],
        in_specs=[pl.BlockSpec(memory_space=pltpu.SMEM)] + [vm] * 6,
        out_specs=[vm] * 3,
        scratch_shapes=[
            pltpu.VMEM((16, 16, 128), F32),
            pltpu.VMEM((8, 16, 128), F32),
            pltpu.VMEM((4, 8, 16, 128), F32),
            pltpu.VMEM((2048, HD), BF),
            pltpu.VMEM((2048, HD), BF),
            pltpu.VMEM((256, 256), BF),
            pltpu.VMEM((16, 2, 64, 256), BF),
            pltpu.VMEM((256, 256), BF),
            pltpu.VMEM((256, D), BF),
            pltpu.VMEM((16, 16, D), BF),
            dma((16,)), dma((16,)),
            dma((4,)), dma((4,)),
            dma((5,)),
            dma((3, 16)), dma((3, 16)),
            dma((16,)), dma((16,)),
            dma, dma,
            dma((16,)), dma((16,)),
        ],
        compiler_params=pltpu.CompilerParams(collective_id=0, has_side_effects=True),
    )(cached_len, kv, q, wt, x, gain, mark)


ORDER = (0, 1, 7, 2, 6, 3, 5, 4)
PLACE = {o: i for i, o in enumerate(ORDER)}
CHUNKS = ((0, 1), (7, 2), (6, 3), (5, 4))


def experts_kernel(
    normed_ref, res_ref, table_ref, wg_ref, wd_ref, out_ref,
    tok, comb, xs, xr, po, pr, part, sl, rl, sr, rr, fs, fr,
    z_send, z_recv, y_send, y_recv, x_send, x_recv, b_send, b_recv, r_send, r_recv, f_send, f_recv,
):
    x, y, z, c = coords()
    q = x * 2 + c
    seq, zhi = (z % 2) * 8 + y, z // 2
    right, left = device(x, lax.rem(y + 1, 8), z, c), device(x, lax.rem(y + 7, 8), z, c)

    def at_q(j):
        n = lax.rem(q + j, 8)
        return device(n // 2, y, z, lax.rem(n, 2))

    def at_z(i):
        return device(x, y, lax.rem(z + i, 8), c)

    greet([at_z(i) for i in range(1, 8)] + [right, left] + [at_q(j) for j in range(1, 8)])

    where_z = {r: (ch, zz) for ch, rs in enumerate(CHUNKS) for zz, r in enumerate(rs)}

    def z_copy(r):
        ch, zz = where_z[r]
        return remote(
            normed_ref, tok.at[ch, 0, zz * 16 : zz * 16 + 16], z_send.at[r], z_recv.at[r], at_z(r)
        )

    def half(h):
        return pl.ds(h * 1024, 1024)

    def whole():
        return pl.ds(0, D)

    def y_copy(way, t, ch):
        a, b, dev = (t, t + 1, right) if way == 0 else ((8 - t) % 8, 7 - t, left)
        cols = whole() if t < 3 else half(way)
        return remote(
            tok.at[ch, PLACE[a], :, cols], tok.at[ch, PLACE[b], :, cols],
            y_send.at[way, t, ch], y_recv.at[way, t, ch], dev,
        )

    def r_copy(way, t, ch):
        src, dst, dev = (sl, rl, left) if way == 0 else (sr, rr, right)
        cols = whole() if t > 0 else half(way)
        return remote(
            src.at[ch, t, :, cols], dst.at[ch, t, :, cols],
            r_send.at[way, t, ch], r_recv.at[way, t, ch], dev,
        )

    def x_copy(u, j):
        return remote(xs.at[u, j], xr.at[u, j], x_send.at[u, j], x_recv.at[u, j], at_q(j))

    def b_copy(u, j):
        return remote(po.at[u, j], pr.at[u, j], b_send.at[u, j], b_recv.at[u, j], at_q(8 - j))

    def f_copy(r):
        ch, zz = where_z[r]
        return remote(
            fs.at[ch, zz * 16 : zz * 16 + 16], fr.at[r], f_send.at[r], f_recv.at[r], at_z(8 - r)
        )

    def gather(ch, t):
        if t == 0:
            for r in CHUNKS[ch]:
                if r:
                    z_copy(r).wait_recv()
        for way in range(2):
            if t > 0:
                y_copy(way, t - 1, ch).wait_recv()
            if t < 4:
                y_copy(way, t, ch).start()

    def select(ch, g):
        u = 2 * ch + g
        lane = lax.broadcasted_iota(jnp.int32, (16, 128), 1)
        table = jnp.zeros((16, 128), F32)
        for p in range(4):
            y0 = lax.rem(y + 8 - ORDER[4 * g + p], 8)
            for zz in range(2):
                z0 = lax.rem(z + 8 - CHUNKS[ch][zz], 8)
                n = 2 * p + zz
                rolled = pltpu.roll(table_ref[y0], lax.rem(n * 16 + 128 - z0 * 16, 128), 1)
                table = jnp.where((lane >> 4) == n, rolled, table)
        row = lax.broadcasted_iota(jnp.int32, (128, 128), 0)
        col = lax.broadcasted_iota(jnp.int32, (128, 128), 1)
        expert = (4 * (zhi * 8 + ((q + (row >> 4)) & 7)) + seq // 4).astype(F32)
        same = ((row >> 1) & 7) == (col >> 4)
        match = jnp.zeros((128, 128), F32)
        gate = jnp.zeros((128, 128), F32)
        for k in range(8):
            hit = same & (table[k : k + 1, :] == expert)
            match = jnp.where(hit, 1.0, match)
            gate = jnp.where(hit, table[8 + k : 9 + k, :], gate)
        before = jnp.where(row < col, 1.0, 0.0).astype(BF)
        rank = jnp.dot(match.astype(BF), before, preferred_element_type=F32)
        pick = jnp.where(rank == (row & 1).astype(F32), match, 0.0)
        comb[u] = (pick * gate).T.astype(BF)
        pick = pick.astype(BF)

        def tile(n, _):
            cols = pl.ds(pl.multiple_of(n * 512, 512), 512)
            rows = tok[ch, 4 * g : 4 * g + 4, :, cols].reshape(128, 512)
            rows = jnp.dot(pick, rows, preferred_element_type=F32).astype(BF)
            xs[u, :, :, cols] = rows.reshape(8, 16, 512)
            xr[u, 0, :, cols] = rows[:16]
            return 0

        lax.fori_loop(0, 4, tile, 0)

        def send(j, _):
            x_copy(u, j).start()
            return 0

        lax.fori_loop(1, 8, send, 0)

    def feed(ch, g):
        u = 2 * ch + g

        def arrive(j, _):
            x_copy(u, j).wait_recv()
            return 0

        lax.fori_loop(1, 8, arrive, 0)
        both = jnp.dot(xr[u].reshape(128, D), wg_ref[...], preferred_element_type=F32)
        v, w = both[:, :192], both[:, 192:]
        hidden = (v / (1.0 + jnp.exp(-v)) * w).astype(BF)

        def tile(n, _):
            cols = pl.ds(pl.multiple_of(n * 512, 512), 512)
            rows = jnp.dot(hidden, wd_ref[:, cols], preferred_element_type=F32).astype(BF)
            po[u, :, :, cols] = rows.reshape(8, 16, 512)
            pr[u, 0, :, cols] = rows[:16]
            return 0

        lax.fori_loop(0, 4, tile, 0)

        def send(j, _):
            b_copy(u, j).start()
            return 0

        lax.fori_loop(1, 8, send, 0)

    def combine(ch, g):
        u = 2 * ch + g

        def arrive(j, _):
            b_copy(u, j).wait_recv()
            return 0

        lax.fori_loop(1, 8, arrive, 0)

        def tile(n, _):
            cols = pl.ds(pl.multiple_of(n * 512, 512), 512)
            rows = pr[u, :, :, cols].reshape(128, 512)
            rows = jnp.dot(comb[u], rows, preferred_element_type=F32)
            part[ch, 4 * g : 4 * g + 4, :, cols] = rows.reshape(4, 32, 512)
            return 0

        lax.fori_loop(0, 4, tile, 0)

    def scatter(ch, t):
        for way in range(2):
            o = 4 - t if way == 0 else 4 + t
            src, dst = (sl, rl) if way == 0 else (sr, rr)
            if t > 0:
                r_copy(way, t - 1, ch).wait_recv()
            for h in range(2):
                if t == 0 and h != way:
                    continue
                value = part[ch, PLACE[o], :, half(h)]
                if t > 1 or (t == 1 and h == way):
                    value = value + dst[ch, t - 1, :, half(h)].astype(F32)
                src[ch, t, :, half(h)] = value.astype(BF)
            r_copy(way, t, ch).start()

    def finish(ch):
        for way in range(2):
            r_copy(way, 3, ch).wait_recv()
        for h in range(2):
            value = part[ch, 0, :, half(h)] + rl[ch, 3, :, half(h)].astype(F32)
            fs[ch, :, half(h)] = (value + rr[ch, 3, :, half(h)].astype(F32)).astype(BF)
        for r in CHUNKS[ch]:
            if r:
                f_copy(r).start()

    for r in (1, 7, 2, 6, 3, 5, 4):
        z_copy(r).start()
    tok[0, 0, :16] = normed_ref[...]

    gather(0, 0)
    gather(0, 1)
    gather(1, 0)
    gather(0, 2)
    select(0, 0)
    gather(1, 1)
    gather(0, 3)
    gather(1, 2)
    gather(0, 4)
    select(0, 1)
    gather(1, 3)
    gather(1, 4)
    for ch in range(5):
        if ch + 2 < 4:
            gather(ch + 2, 0)
        if ch + 1 < 4:
            select(ch + 1, 0)
        if ch < 4:
            feed(ch, 0)
        if ch + 2 < 4:
            gather(ch + 2, 1)
        if ch + 1 < 4:
            select(ch + 1, 1)
        if ch > 0:
            combine(ch - 1, 1)
            scatter(ch - 1, 0)
        if ch < 4:
            feed(ch, 1)
        if ch + 2 < 4:
            gather(ch + 2, 2)
        if ch > 0:
            combine(ch - 1, 0)
            scatter(ch - 1, 1)
        if ch + 2 < 4:
            gather(ch + 2, 3)
        if ch > 0:
            scatter(ch - 1, 2)
        if ch + 2 < 4:
            gather(ch + 2, 4)
        if ch > 0:
            scatter(ch - 1, 3)
            finish(ch - 1)

    acc = res_ref[...].astype(F32) + fs[0, :16].astype(F32)
    for r in (1, 7, 2, 6, 3, 5, 4):
        f_copy(r).wait_recv()
        acc = acc + fr[r].astype(F32)
    out_ref[...] = acc.astype(BF)

    for r in range(1, 8):
        z_copy(r).wait_send()
        f_copy(r).wait_send()
    for ch in range(4):
        for t in range(4):
            for way in range(2):
                y_copy(way, t, ch).wait_send()
                r_copy(way, t, ch).wait_send()

    def sent(u, _):
        def one(j, _):
            x_copy(u, j).wait_send()
            b_copy(u, j).wait_send()
            return 0

        return lax.fori_loop(1, 8, one, 0)

    lax.fori_loop(0, 8, sent, 0)


def experts(normed, residual, table, wg, wd):
    vm = pl.BlockSpec(memory_space=pltpu.VMEM)
    dma = pltpu.SemaphoreType.DMA
    big = pltpu.VMEM((8, 8, 16, D), BF)
    hop = pltpu.VMEM((4, 4, 32, D), BF)
    return pl.pallas_call(
        experts_kernel,
        name="experts",
        out_shape=jax.ShapeDtypeStruct((16, D), BF),
        in_specs=[vm] * 5,
        out_specs=vm,
        scratch_shapes=[
            pltpu.VMEM((4, 8, 32, D), BF),
            pltpu.VMEM((8, 128, 128), BF),
            big, big, big, big,
            pltpu.VMEM((4, 8, 32, D), F32),
            hop, hop, hop, hop,
            pltpu.VMEM((4, 32, D), BF),
            pltpu.VMEM((8, 16, D), BF),
            dma((8,)), dma((8,)),
            dma((2, 4, 4)), dma((2, 4, 4)),
            dma((8, 8)), dma((8, 8)),
            dma((8, 8)), dma((8, 8)),
            dma((2, 4, 4)), dma((2, 4, 4)),
            dma((8,)), dma((8,)),
        ],
        compiler_params=pltpu.CompilerParams(
            collective_id=1, has_side_effects=True, vmem_limit_bytes=56 * 1024 * 1024
        ),
    )(normed, residual, table, wg, wd)


def local(
    layer_input, queries, fresh_kv, cache_kv, cached_len, out_weight, norm_gain,
    routes, route_gates, w_gate_up, w_down,
):
    z = coords()[2]
    mark = jnp.concatenate([routes[0].T.astype(F32), route_gates[0].T], 0)
    mark = jnp.where(jnp.arange(128)[None] // 16 == z, jnp.tile(mark, (1, 8)), 0.0)
    kv = jnp.concatenate([cache_kv[0], fresh_kv[0]], 0)
    residual, normed, table = attention(
        cached_len, kv, queries[0], out_weight.T, layer_input[0], norm_gain[None], mark
    )
    return experts(normed, residual, table, w_gate_up[0], w_down[0])[None]


def solution(mesh):
    return jax.shard_map(
        local,
        mesh=mesh,
        in_specs=(
            P("req", "seq", None),
            P("req", "seq", None),
            P("req", "seq", None),
            P("req", "seq", None),
            P("req"),
            P("seq", "req"),
            P(),
            P("req", "seq", None),
            P("req", "seq", None),
            P(("req", "seq"), None, None),
            P(("req", "seq"), None, None),
        ),
        out_specs=P("req", "seq", None),
        check_vma=False,
    )
```

```python
import math

import jax
import jax.numpy as jnp
from jax import lax
from jax.experimental import pallas as pl
from jax.experimental.pallas import tpu as pltpu
from jax.sharding import PartitionSpec as P

MESH = pl.DeviceIdType.MESH
BF = jnp.bfloat16
F32 = jnp.float32
NEG = -1e30
EPS = 1e-06
D = 2048
HD = 128
NT = (((1,), (1,)), ((), ()))


def coords():
    req, seq = lax.axis_index("req"), lax.axis_index("seq")
    z = (req // 8) * 2 + seq // 8
    return (req // 2) % 4, seq % 8, z, req % 2


def device(x, y, z, c):
    return ((z // 2) * 8 + x * 2 + c, (z % 2) * 8 + y)


def remote(src, dst, send, recv, dev):
    return pltpu.make_async_remote_copy(
        src_ref=src, dst_ref=dst, send_sem=send, recv_sem=recv, device_id=dev, device_id_type=MESH
    )


def greet(devs):
    barrier = pltpu.get_barrier_semaphore()
    for dev in devs:
        pl.semaphore_signal(barrier, inc=1, device_id=dev, device_id_type=MESH)
    pl.semaphore_wait(barrier, len(devs))


def attention_kernel(
    len_ref, kv_ref, q_ref, wt_ref, x_ref, gain_ref, mark_ref, res_ref, normed_ref, table_ref,
    marks, near, far, kbuf, vbuf, qbuf, wbuf, att, pbuf, rbuf,
    m_send, m_recv, n_send, n_recv, own_sem, kv_send, kv_recv, w_send, w_recv, sib_send, sib_recv, p_send, p_recv,
):
    req, seq = lax.axis_index("req"), lax.axis_index("seq")
    m, c = req // 2, req % 2
    peers = [(req, lax.rem(seq + i, 16)) for i in range(1, 16)]
    chips = [(lax.rem(m + i, 16) * 2 + c, seq) for i in range(1, 16)]
    sibling = (m * 2 + 1 - c, seq)
    greet(peers + chips + [sibling])

    def piece(part, dst_seq, src_seq, i):
        rows = pl.ds(pl.multiple_of(src_seq * 128, 128), 128)
        head = dst_seq // 4
        if part == 0:
            cols = pl.ds(pl.multiple_of(head * HD, HD), HD)
            return kv_ref.at[:, cols], kbuf.at[rows, :]
        if part == 1:
            cols = pl.ds(pl.multiple_of(512 + head * HD, HD), HD)
            return kv_ref.at[:, cols], vbuf.at[rows, :]
        rows = pl.ds(pl.multiple_of(src_seq * 16, 16), 16)
        cols = pl.ds(pl.multiple_of(dst_seq * 256, 256), 256)
        return q_ref.at[:, cols], qbuf.at[rows, :]

    def kv_copy(part, i):
        dst_seq = lax.rem(seq + i, 16)
        src, dst = piece(part, dst_seq, seq, i)
        return remote(src, dst, kv_send.at[part, i], kv_recv.at[part, i], (req, dst_seq))

    def w_copy(i):
        return remote(
            wt_ref, wbuf.at[m, c], w_send.at[i], w_recv.at[i], (lax.rem(m + i, 16) * 2 + c, seq)
        )

    def mark_copy(i):
        dst_seq = lax.rem(seq + i, 16)
        return remote(mark_ref, marks.at[seq], m_send.at[i], m_recv.at[i], (req, dst_seq))

    def near_copy(i):
        dst = (lax.rem(req + 8 * i, 32), seq)
        return remote(near, far.at[i], n_send.at[i], n_recv.at[i], dst)

    def mark_wait(i, _):
        mark_copy(i).wait()
        return 0

    def start(i, _):
        mark_copy(i).start()
        for part in range(3):
            kv_copy(part, i).start()
        w_copy(i).start()
        return 0

    lax.fori_loop(1, 16, start, 0)
    own = []
    for part in range(3):
        src, dst = piece(part, seq, seq, 0)
        own.append(pltpu.make_async_copy(src, dst, own_sem.at[part]))
    own.append(pltpu.make_async_copy(wt_ref, wbuf.at[m, c], own_sem.at[3]))
    own.append(pltpu.make_async_copy(mark_ref, marks.at[seq], own_sem.at[4]))
    for copy in own:
        copy.start()
    for copy in own:
        copy.wait()

    def kv_wait(i, _):
        for part in range(3):
            kv_copy(part, i).wait()
        return 0

    def w_wait(i, _):
        w_copy(i).wait()
        return 0

    lax.fori_loop(1, 16, mark_wait, 0)
    for n in range(8):
        near[n] = marks[n] + marks[8 + n]
    for i in range(1, 4):
        near_copy(i).start()
    lax.fori_loop(1, 16, w_wait, 0)
    sib = remote(wbuf.at[:, c], wbuf.at[:, c], sib_send, sib_recv, sibling)
    sib.start()
    lax.fori_loop(1, 16, kv_wait, 0)

    length = len_ref[0]
    scale = 1.0 / math.sqrt(HD)
    sib.wait()

    def p_copy(dst_seq):
        i = lax.rem(dst_seq + 16 - seq, 16)
        rows = pl.ds(pl.multiple_of(dst_seq * 16, 16), 16)
        return remote(pbuf.at[rows, :], rbuf.at[i], p_send.at[i], p_recv.at[i], (req, dst_seq))

    def tile(step, _):
        quad = lax.rem(seq // 4 + 1 + step, 4)
        rows = pl.ds(pl.multiple_of(quad * 64, 64), 64)
        for head in range(2):
            q = qbuf[rows, head * HD : (head + 1) * HD]
            s = lax.dot_general(q, kbuf[...], NT, preferred_element_type=F32) * scale
            col = lax.broadcasted_iota(jnp.int32, (64, D), 1)
            tok = lax.broadcasted_iota(jnp.int32, (64, D), 0) + quad * 64
            src, within = col >> 7, col & 127
            behind = jnp.where(
                within < 112, src * 112 + within - length, src * 16 + within - 113 - tok
            )
            seen = behind < 0
            s = jnp.where(seen, s, NEG)
            w = jnp.where(seen, jnp.exp(s - jnp.max(s, axis=-1, keepdims=True)), 0.0)
            total = jnp.sum(w, axis=-1, keepdims=True)
            mixed = jnp.dot(w.astype(BF), vbuf[...], preferred_element_type=F32)
            att[rows, head * HD : (head + 1) * HD] = (mixed / total).astype(BF)

        def project(i, _):
            w = wbuf[pl.ds(i * 4, 4)].reshape(512, 256)
            cols = pl.ds(pl.multiple_of(i * 512, 512), 512)
            out = lax.dot_general(att[rows, :], w, NT, preferred_element_type=F32)
            pbuf[rows, cols] = out.astype(BF)
            return 0

        lax.fori_loop(0, 4, project, 0)

        def send(n, _):
            dst_seq = quad * 4 + lax.rem(seq + n, 4)

            @pl.when(dst_seq != seq)
            def _():
                p_copy(dst_seq).start()

            return 0

        return lax.fori_loop(0, 4, send, 0)

    lax.fori_loop(0, 4, tile, 0)

    def p_wait(i, _):
        p_copy(lax.rem(seq + i, 16)).wait()
        return 0

    for i in range(1, 4):
        near_copy(i).wait()
    for n in range(8):
        table_ref[n] = near[n] + far[1, n] + far[2, n] + far[3, n]
    rbuf[0] = pbuf[pl.ds(pl.multiple_of(seq * 16, 16), 16), :]
    lax.fori_loop(1, 16, p_wait, 0)
    projected = lax.fori_loop(
        0, 16, lambda i, acc: acc + rbuf[i].astype(F32), jnp.zeros((16, D), F32)
    )
    residual = (x_ref[...].astype(F32) + projected).astype(BF)
    res_ref[...] = residual
    r = residual.astype(F32)
    mean = jnp.mean(r * r, axis=-1, keepdims=True)
    normed_ref[...] = (r * lax.rsqrt(mean + EPS) * gain_ref[...]).astype(BF)


def attention(cached_len, kv, q, wt, x, gain, mark):
    vm = pl.BlockSpec(memory_space=pltpu.VMEM)
    dma = pltpu.SemaphoreType.DMA
    return pl.pallas_call(
        attention_kernel,
        name="attention",
        out_shape=[jax.ShapeDtypeStruct((16, D), BF)] * 2
        + [jax.ShapeDtypeStruct((8, 16, 128), F32)],
        in_specs=[pl.BlockSpec(memory_space=pltpu.SMEM)] + [vm] * 6,
        out_specs=[vm] * 3,
        scratch_shapes=[
            pltpu.VMEM((16, 16, 128), F32),
            pltpu.VMEM((8, 16, 128), F32),
            pltpu.VMEM((4, 8, 16, 128), F32),
            pltpu.VMEM((2048, HD), BF),
            pltpu.VMEM((2048, HD), BF),
            pltpu.VMEM((256, 256), BF),
            pltpu.VMEM((16, 2, 64, 256), BF),
            pltpu.VMEM((256, 256), BF),
            pltpu.VMEM((256, D), BF),
            pltpu.VMEM((16, 16, D), BF),
            dma((16,)), dma((16,)),
            dma((4,)), dma((4,)),
            dma((5,)),
            dma((3, 16)), dma((3, 16)),
            dma((16,)), dma((16,)),
            dma, dma,
            dma((16,)), dma((16,)),
        ],
        compiler_params=pltpu.CompilerParams(collective_id=0, has_side_effects=True),
    )(cached_len, kv, q, wt, x, gain, mark)


ORDER = (0, 1, 7, 2, 6, 3, 5, 4)
PLACE = {o: i for i, o in enumerate(ORDER)}
CHUNKS = ((0, 1), (7, 2), (6, 3), (5, 4))

PLAN = (
    ("g", 0, 0),
    ("g", 1, 0),
    ("g", 0, 1),
    ("g", 1, 1),
    ("g", 0, 2),
    ("s", 0, 0),
    ("g", 1, 2),
    ("g", 2, 0),
    ("s", 1, 0),
    ("g", 1, 3),
    ("g", 0, 3),
    ("g", 3, 0),
    ("f", 0, 0),
    ("g", 1, 4),
    ("g", 0, 4),
    ("g", 2, 1),
    ("s", 0, 1),
    ("g", 3, 1),
    ("g", 2, 2),
    ("s", 1, 1),
    ("g", 2, 3),
    ("f", 0, 1),
    ("f", 1, 1),
    ("g", 2, 4),
    ("c", 0, 1),
    ("g", 3, 2),
    ("s", 2, 1),
    ("g", 3, 3),
    ("f", 1, 0),
    ("c", 1, 1),
    ("s", 2, 0),
    ("r", 0, 0),
    ("g", 3, 4),
    ("r", 1, 0),
    ("s", 3, 1),
    ("c", 1, 0),
    ("r", 0, 1),
    ("c", 0, 0),
    ("r", 1, 1),
    ("s", 3, 0),
    ("f", 3, 1),
    ("r", 0, 2),
    ("r", 1, 2),
    ("f", 2, 1),
    ("f", 3, 0),
    ("r", 1, 3),
    ("f", 2, 0),
    ("c", 3, 1),
    ("r", 3, 0),
    ("r", 0, 3),
    ("c", 2, 1),
    ("r", 2, 0),
    ("r", 3, 1),
    ("n", 1, 0),
    ("r", 2, 1),
    ("c", 3, 0),
    ("r", 3, 2),
    ("c", 2, 0),
    ("r", 2, 2),
    ("r", 3, 3),
    ("r", 2, 3),
    ("n", 0, 0),
    ("n", 3, 0),
    ("n", 2, 0),
)


def experts_kernel(
    normed_ref, res_ref, table_ref, wg_ref, wd_ref, out_ref,
    tok, comb, xs, xr, po, pr, part, sl, rl, sr, rr, fs, fr,
    z_send, z_recv, y_send, y_recv, x_send, x_recv, b_send, b_recv, r_send, r_recv, f_send, f_recv,
):
    x, y, z, c = coords()
    seq, zhi = (z % 2) * 8 + y, z // 2
    right, left = device(x, lax.rem(y + 1, 8), z, c), device(x, lax.rem(y + 7, 8), z, c)

    def at_x(j, back=False):
        far = 4 - j // 2 if back else j // 2
        return device(lax.rem(x + far, 4), y, z, lax.rem(c + j, 2))

    def at_z(i):
        return device(x, y, lax.rem(z + i, 8), c)

    greet([at_z(i) for i in range(1, 8)] + [right, left] + [at_x(j) for j in range(1, 8)])

    where_z = {r: (ch, zz) for ch, rs in enumerate(CHUNKS) for zz, r in enumerate(rs)}

    def z_copy(r):
        ch, zz = where_z[r]
        return remote(
            normed_ref, tok.at[ch, 0, zz * 16 : zz * 16 + 16], z_send.at[r], z_recv.at[r], at_z(r)
        )

    def half(h):
        return pl.ds(h * 1024, 1024)

    def whole():
        return pl.ds(0, D)

    def y_copy(way, t, ch):
        a, b, dev = (t, t + 1, right) if way == 0 else ((8 - t) % 8, 7 - t, left)
        cols = whole() if t < 3 else half(way)
        return remote(
            tok.at[ch, PLACE[a], :, cols], tok.at[ch, PLACE[b], :, cols],
            y_send.at[way, t, ch], y_recv.at[way, t, ch], dev,
        )

    def r_copy(way, t, ch):
        src, dst, dev = (sl, rl, left) if way == 0 else (sr, rr, right)
        cols = whole() if t > 0 else half(way)
        return remote(
            src.at[ch, t, :, cols], dst.at[ch, t, :, cols],
            r_send.at[way, t, ch], r_recv.at[way, t, ch], dev,
        )

    def x_copy(u, j):
        return remote(xs.at[u, j], xr.at[u, j], x_send.at[u, j], x_recv.at[u, j], at_x(j))

    def b_copy(u, j):
        return remote(po.at[u, j], pr.at[u, j], b_send.at[u, j], b_recv.at[u, j], at_x(j, True))

    def f_copy(r):
        ch, zz = where_z[r]
        return remote(
            fs.at[ch, zz * 16 : zz * 16 + 16], fr.at[r], f_send.at[r], f_recv.at[r], at_z(8 - r)
        )

    def gather(ch, t):
        if t == 0:
            for r in CHUNKS[ch]:
                if r:
                    z_copy(r).wait_recv()
        for way in range(2):
            if t > 0:
                y_copy(way, t - 1, ch).wait_recv()
            if t < 4:
                y_copy(way, t, ch).start()

    def select(ch, g):
        u = 2 * ch + g
        lane = lax.broadcasted_iota(jnp.int32, (16, 128), 1)
        table = jnp.zeros((16, 128), F32)
        for p in range(4):
            y0 = lax.rem(y + 8 - ORDER[4 * g + p], 8)
            for zz in range(2):
                z0 = lax.rem(z + 8 - CHUNKS[ch][zz], 8)
                n = 2 * p + zz
                rolled = pltpu.roll(table_ref[y0], lax.rem(n * 16 + 128 - z0 * 16, 128), 1)
                table = jnp.where((lane >> 4) == n, rolled, table)
        row = lax.broadcasted_iota(jnp.int32, (128, 128), 0)
        col = lax.broadcasted_iota(jnp.int32, (128, 128), 1)
        req = zhi * 8 + ((x + (row >> 5)) & 3) * 2 + ((c + (row >> 4)) & 1)
        expert = (4 * req + seq // 4).astype(F32)
        same = ((row >> 1) & 7) == (col >> 4)
        match = jnp.zeros((128, 128), F32)
        gate = jnp.zeros((128, 128), F32)
        for k in range(8):
            hit = same & (table[k : k + 1, :] == expert)
            match = jnp.where(hit, 1.0, match)
            gate = jnp.where(hit, table[8 + k : 9 + k, :], gate)
        before = jnp.where(row < col, 1.0, 0.0).astype(BF)
        rank = jnp.dot(match.astype(BF), before, preferred_element_type=F32)
        pick = jnp.where(rank == (row & 1).astype(F32), match, 0.0)
        comb[u] = (pick * gate).T.astype(BF)
        pick = pick.astype(BF)

        def tile(n, _):
            cols = pl.ds(pl.multiple_of(n * 512, 512), 512)
            rows = tok[ch, 4 * g : 4 * g + 4, :, cols].reshape(128, 512)
            rows = jnp.dot(pick, rows, preferred_element_type=F32).astype(BF)
            xs[u, :, :, cols] = rows.reshape(8, 16, 512)
            xr[u, 0, :, cols] = rows[:16]
            return 0

        lax.fori_loop(0, 4, tile, 0)

        def send(j, _):
            x_copy(u, j).start()
            return 0

        lax.fori_loop(1, 8, send, 0)

    def feed(ch, g):
        u = 2 * ch + g

        def arrive(j, _):
            x_copy(u, j).wait_recv()
            return 0

        lax.fori_loop(1, 8, arrive, 0)
        both = jnp.dot(xr[u].reshape(128, D), wg_ref[...], preferred_element_type=F32)
        v, w = both[:, :192], both[:, 192:]
        hidden = (v / (1.0 + jnp.exp(-v)) * w).astype(BF)

        def tile(n, _):
            cols = pl.ds(pl.multiple_of(n * 512, 512), 512)
            rows = jnp.dot(hidden, wd_ref[:, cols], preferred_element_type=F32).astype(BF)
            po[u, :, :, cols] = rows.reshape(8, 16, 512)
            pr[u, 0, :, cols] = rows[:16]
            return 0

        lax.fori_loop(0, 4, tile, 0)

        def send(j, _):
            b_copy(u, j).start()
            return 0

        lax.fori_loop(1, 8, send, 0)

    def combine(ch, g):
        u = 2 * ch + g

        def arrive(j, _):
            b_copy(u, j).wait_recv()
            return 0

        lax.fori_loop(1, 8, arrive, 0)

        def tile(n, _):
            cols = pl.ds(pl.multiple_of(n * 512, 512), 512)
            rows = pr[u, :, :, cols].reshape(128, 512)
            rows = jnp.dot(comb[u], rows, preferred_element_type=F32)
            part[ch, 4 * g : 4 * g + 4, :, cols] = rows.reshape(4, 32, 512)
            return 0

        lax.fori_loop(0, 4, tile, 0)

    def scatter(ch, t):
        for way in range(2):
            o = 4 - t if way == 0 else 4 + t
            src, dst = (sl, rl) if way == 0 else (sr, rr)
            if t > 0:
                r_copy(way, t - 1, ch).wait_recv()
            for h in range(2):
                if t == 0 and h != way:
                    continue
                value = part[ch, PLACE[o], :, half(h)]
                if t > 1 or (t == 1 and h == way):
                    value = value + dst[ch, t - 1, :, half(h)].astype(F32)
                src[ch, t, :, half(h)] = value.astype(BF)
            r_copy(way, t, ch).start()

    def finish(ch):
        for way in range(2):
            r_copy(way, 3, ch).wait_recv()
        for h in range(2):
            value = part[ch, 0, :, half(h)] + rl[ch, 3, :, half(h)].astype(F32)
            fs[ch, :, half(h)] = (value + rr[ch, 3, :, half(h)].astype(F32)).astype(BF)
        for r in CHUNKS[ch]:
            if r:
                f_copy(r).start()

    for r in (1, 7, 2, 6, 3, 5, 4):
        z_copy(r).start()
    tok[0, 0, :16] = normed_ref[...]

    work = {"g": gather, "s": select, "f": feed, "c": combine, "r": scatter, "n": lambda ch, _: finish(ch)}
    for kind, ch, i in PLAN:
        work[kind](ch, i)

    acc = res_ref[...].astype(F32) + fs[0, :16].astype(F32)
    for r in (1, 7, 2, 6, 3, 5, 4):
        f_copy(r).wait_recv()
        acc = acc + fr[r].astype(F32)
    out_ref[...] = acc.astype(BF)

    for r in range(1, 8):
        z_copy(r).wait_send()
        f_copy(r).wait_send()
    for ch in range(4):
        for t in range(4):
            for way in range(2):
                y_copy(way, t, ch).wait_send()
                r_copy(way, t, ch).wait_send()

    def sent(u, _):
        def one(j, _):
            x_copy(u, j).wait_send()
            b_copy(u, j).wait_send()
            return 0

        return lax.fori_loop(1, 8, one, 0)

    lax.fori_loop(0, 8, sent, 0)


def experts(normed, residual, table, wg, wd):
    vm = pl.BlockSpec(memory_space=pltpu.VMEM)
    dma = pltpu.SemaphoreType.DMA
    big = pltpu.VMEM((8, 8, 16, D), BF)
    hop = pltpu.VMEM((4, 4, 32, D), BF)
    return pl.pallas_call(
        experts_kernel,
        name="experts",
        out_shape=jax.ShapeDtypeStruct((16, D), BF),
        in_specs=[vm] * 5,
        out_specs=vm,
        scratch_shapes=[
            pltpu.VMEM((4, 8, 32, D), BF),
            pltpu.VMEM((8, 128, 128), BF),
            big, big, big, big,
            pltpu.VMEM((4, 8, 32, D), F32),
            hop, hop, hop, hop,
            pltpu.VMEM((4, 32, D), BF),
            pltpu.VMEM((8, 16, D), BF),
            dma((8,)), dma((8,)),
            dma((2, 4, 4)), dma((2, 4, 4)),
            dma((8, 8)), dma((8, 8)),
            dma((8, 8)), dma((8, 8)),
            dma((2, 4, 4)), dma((2, 4, 4)),
            dma((8,)), dma((8,)),
        ],
        compiler_params=pltpu.CompilerParams(
            collective_id=1, has_side_effects=True, vmem_limit_bytes=56 * 1024 * 1024
        ),
    )(normed, residual, table, wg, wd)


def local(
    layer_input, queries, fresh_kv, cache_kv, cached_len, out_weight, norm_gain,
    routes, route_gates, w_gate_up, w_down,
):
    z = coords()[2]
    mark = jnp.concatenate([routes[0].T.astype(F32), route_gates[0].T], 0)
    mark = jnp.where(jnp.arange(128)[None] // 16 == z, jnp.tile(mark, (1, 8)), 0.0)
    kv = jnp.concatenate([cache_kv[0], fresh_kv[0]], 0)
    residual, normed, table = attention(
        cached_len, kv, queries[0], out_weight.T, layer_input[0], norm_gain[None], mark
    )
    return experts(normed, residual, table, w_gate_up[0], w_down[0])[None]


def solution(mesh):
    return jax.shard_map(
        local,
        mesh=mesh,
        in_specs=(
            P("req", "seq", None),
            P("req", "seq", None),
            P("req", "seq", None),
            P("req", "seq", None),
            P("req"),
            P("seq", "req"),
            P(),
            P("req", "seq", None),
            P("req", "seq", None),
            P(("req", "seq"), None, None),
            P(("req", "seq"), None, None),
        ),
        out_specs=P("req", "seq", None),
        check_vma=False,
    )
```

```python
import functools
import math

import jax
import jax.numpy as jnp
from jax import lax
from jax.experimental import pallas as pl
from jax.experimental.pallas import tpu as pltpu
from jax.sharding import PartitionSpec as P

MESH = pl.DeviceIdType.MESH
BF = jnp.bfloat16
F32 = jnp.float32
NEG = -1e30
EPS = 1e-06
D = 2048
HD = 128
NT = (((1,), (1,)), ((), ()))


def coords():
    req, seq = lax.axis_index("req"), lax.axis_index("seq")
    z = (req // 8) * 2 + seq // 8
    return (req // 2) % 4, seq % 8, z, req % 2


def device(x, y, z, c):
    return ((z // 2) * 8 + x * 2 + c, (z % 2) * 8 + y)


def remote(src, dst, send, recv, dev):
    return pltpu.make_async_remote_copy(
        src_ref=src, dst_ref=dst, send_sem=send, recv_sem=recv, device_id=dev, device_id_type=MESH
    )


def greet(devs):
    barrier = pltpu.get_barrier_semaphore()
    for dev in devs:
        pl.semaphore_signal(barrier, inc=1, device_id=dev, device_id_type=MESH)
    pl.semaphore_wait(barrier, len(devs))


def attention_part(
    weights, len_ref, kv_ref, q_ref, wt_ref, x_ref, gain_ref, mark_ref, res_ref, normed_ref, table_ref,
    marks, near, far, kbuf, vbuf, qbuf, wbuf, att, pbuf, rbuf,
    m_send, m_recv, n_send, n_recv, own_sem, kv_send, kv_recv, w_send, w_recv, sib_send, sib_recv, p_send, p_recv,
):
    req, seq = lax.axis_index("req"), lax.axis_index("seq")
    m, c = req // 2, req % 2
    peers = [(req, lax.rem(seq + i, 16)) for i in range(1, 16)]
    chips = [(lax.rem(m + i, 16) * 2 + c, seq) for i in range(1, 16)]
    sibling = (m * 2 + 1 - c, seq)
    x, y, z, _ = coords()
    across = [device(lax.rem(x + i, 4), y, z, 1 - c) for i in range(1, 4)]
    along = [device(x, y, lax.rem(z + i, 8), c) for i in range(1, 8)]
    greet(peers + chips + [sibling] + across + along)
    for copy in weights:
        copy.start()

    def piece(part, dst_seq, src_seq, i):
        rows = pl.ds(pl.multiple_of(src_seq * 128, 128), 128)
        head = dst_seq // 4
        if part == 0:
            cols = pl.ds(pl.multiple_of(head * HD, HD), HD)
            return kv_ref.at[:, cols], kbuf.at[rows, :]
        if part == 1:
            cols = pl.ds(pl.multiple_of(512 + head * HD, HD), HD)
            return kv_ref.at[:, cols], vbuf.at[rows, :]
        rows = pl.ds(pl.multiple_of(src_seq * 16, 16), 16)
        cols = pl.ds(pl.multiple_of(dst_seq * 256, 256), 256)
        return q_ref.at[:, cols], qbuf.at[rows, :]

    def kv_copy(part, i):
        dst_seq = lax.rem(seq + i, 16)
        src, dst = piece(part, dst_seq, seq, i)
        return remote(src, dst, kv_send.at[part, i], kv_recv.at[part, i], (req, dst_seq))

    def w_copy(i):
        return remote(
            wt_ref, wbuf.at[m, c], w_send.at[i], w_recv.at[i], (lax.rem(m + i, 16) * 2 + c, seq)
        )

    def mark_copy(i):
        dst_seq = lax.rem(seq + i, 16)
        return remote(mark_ref, marks.at[seq], m_send.at[i], m_recv.at[i], (req, dst_seq))

    def near_copy(i):
        dst = (lax.rem(req + 8 * i, 32), seq)
        return remote(near, far.at[i], n_send.at[i], n_recv.at[i], dst)

    def mark_wait(i, _):
        mark_copy(i).wait()
        return 0

    def start(i, _):
        mark_copy(i).start()
        for part in range(3):
            kv_copy(part, i).start()
        w_copy(i).start()
        return 0

    lax.fori_loop(1, 16, start, 0)
    own = []
    for part in range(3):
        src, dst = piece(part, seq, seq, 0)
        own.append(pltpu.make_async_copy(src, dst, own_sem.at[part]))
    own.append(pltpu.make_async_copy(wt_ref, wbuf.at[m, c], own_sem.at[3]))
    own.append(pltpu.make_async_copy(mark_ref, marks.at[seq], own_sem.at[4]))
    for copy in own:
        copy.start()
    for copy in own:
        copy.wait()

    def kv_wait(i, _):
        for part in range(3):
            kv_copy(part, i).wait()
        return 0

    def w_wait(i, _):
        w_copy(i).wait()
        return 0

    lax.fori_loop(1, 16, mark_wait, 0)
    for n in range(8):
        near[n] = marks[n] + marks[8 + n]
    for i in range(1, 4):
        near_copy(i).start()
    lax.fori_loop(1, 16, w_wait, 0)
    sib = remote(wbuf.at[:, c], wbuf.at[:, c], sib_send, sib_recv, sibling)
    sib.start()
    lax.fori_loop(1, 16, kv_wait, 0)

    length = len_ref[0]
    scale = 1.0 / math.sqrt(HD)
    sib.wait()

    def p_copy(dst_seq):
        i = lax.rem(dst_seq + 16 - seq, 16)
        rows = pl.ds(pl.multiple_of(dst_seq * 16, 16), 16)
        return remote(pbuf.at[rows, :], rbuf.at[i], p_send.at[i], p_recv.at[i], (req, dst_seq))

    def tile(step, _):
        quad = lax.rem(seq // 4 + 1 + step, 4)
        rows = pl.ds(pl.multiple_of(quad * 64, 64), 64)
        for head in range(2):
            q = qbuf[rows, head * HD : (head + 1) * HD]
            s = lax.dot_general(q, kbuf[...], NT, preferred_element_type=F32) * scale
            col = lax.broadcasted_iota(jnp.int32, (64, D), 1)
            tok = lax.broadcasted_iota(jnp.int32, (64, D), 0) + quad * 64
            src, within = col >> 7, col & 127
            behind = jnp.where(
                within < 112, src * 112 + within - length, src * 16 + within - 113 - tok
            )
            seen = behind < 0
            s = jnp.where(seen, s, NEG)
            w = jnp.where(seen, jnp.exp(s - jnp.max(s, axis=-1, keepdims=True)), 0.0)
            total = jnp.sum(w, axis=-1, keepdims=True)
            mixed = jnp.dot(w.astype(BF), vbuf[...], preferred_element_type=F32)
            att[rows, head * HD : (head + 1) * HD] = (mixed / total).astype(BF)

        def project(i, _):
            w = wbuf[pl.ds(i * 4, 4)].reshape(512, 256)
            cols = pl.ds(pl.multiple_of(i * 512, 512), 512)
            out = lax.dot_general(att[rows, :], w, NT, preferred_element_type=F32)
            pbuf[rows, cols] = out.astype(BF)
            return 0

        lax.fori_loop(0, 4, project, 0)

        def send(n, _):
            dst_seq = quad * 4 + lax.rem(seq + n, 4)

            @pl.when(dst_seq != seq)
            def _():
                p_copy(dst_seq).start()

            return 0

        return lax.fori_loop(0, 4, send, 0)

    lax.fori_loop(0, 4, tile, 0)

    def p_wait(i, _):
        p_copy(lax.rem(seq + i, 16)).wait()
        return 0

    for i in range(1, 4):
        near_copy(i).wait()
    for n in range(8):
        table_ref[n] = near[n] + far[1, n] + far[2, n] + far[3, n]
    rbuf[0] = pbuf[pl.ds(pl.multiple_of(seq * 16, 16), 16), :]
    lax.fori_loop(1, 16, p_wait, 0)
    projected = lax.fori_loop(
        0, 16, lambda i, acc: acc + rbuf[i].astype(F32), jnp.zeros((16, D), F32)
    )
    residual = (x_ref[...].astype(F32) + projected).astype(BF)
    res_ref[...] = residual
    r = residual.astype(F32)
    mean = jnp.mean(r * r, axis=-1, keepdims=True)
    normed_ref[...] = (r * lax.rsqrt(mean + EPS) * gain_ref[...]).astype(BF)


ORDER = (0, 1, 7, 2, 6, 3, 5, 4)
PLACE = {o: i for i, o in enumerate(ORDER)}
CHUNKS = ((0, 1), (7, 2), (6, 3), (5, 4))

PLAN = (
    ("g", 0, 0),
    ("g", 1, 0),
    ("g", 0, 1),
    ("g", 1, 1),
    ("g", 0, 2),
    ("s", 0, 0),
    ("g", 1, 2),
    ("g", 2, 0),
    ("s", 1, 0),
    ("g", 1, 3),
    ("g", 0, 3),
    ("g", 3, 0),
    ("f", 0, 0),
    ("g", 1, 4),
    ("g", 0, 4),
    ("g", 2, 1),
    ("s", 0, 1),
    ("g", 3, 1),
    ("g", 2, 2),
    ("s", 1, 1),
    ("g", 2, 3),
    ("f", 0, 1),
    ("f", 1, 1),
    ("g", 2, 4),
    ("c", 0, 1),
    ("g", 3, 2),
    ("s", 2, 1),
    ("g", 3, 3),
    ("f", 1, 0),
    ("c", 1, 1),
    ("s", 2, 0),
    ("r", 0, 0),
    ("g", 3, 4),
    ("r", 1, 0),
    ("s", 3, 1),
    ("c", 1, 0),
    ("r", 0, 1),
    ("c", 0, 0),
    ("r", 1, 1),
    ("s", 3, 0),
    ("f", 3, 1),
    ("r", 0, 2),
    ("r", 1, 2),
    ("f", 2, 1),
    ("f", 3, 0),
    ("r", 1, 3),
    ("f", 2, 0),
    ("c", 3, 1),
    ("r", 3, 0),
    ("r", 0, 3),
    ("c", 2, 1),
    ("r", 2, 0),
    ("r", 3, 1),
    ("n", 1, 0),
    ("r", 2, 1),
    ("c", 3, 0),
    ("r", 3, 2),
    ("c", 2, 0),
    ("r", 2, 2),
    ("r", 3, 3),
    ("r", 2, 3),
    ("n", 0, 0),
    ("n", 3, 0),
    ("n", 2, 0),
)


def experts_part(
    weights, normed_ref, res_ref, table_ref, wg_ref, wd_ref, out_ref,
    tok, comb, xs, xr, po, pr, part, sl, rl, sr, rr, fs, fr,
    z_send, z_recv, y_send, y_recv, x_send, x_recv, b_send, b_recv, r_send, r_recv, f_send, f_recv,
):
    x, y, z, c = coords()
    seq, zhi = (z % 2) * 8 + y, z // 2
    right, left = device(x, lax.rem(y + 1, 8), z, c), device(x, lax.rem(y + 7, 8), z, c)

    def at_x(j, back=False):
        far = 4 - j // 2 if back else j // 2
        return device(lax.rem(x + far, 4), y, z, lax.rem(c + j, 2))

    def at_z(i):
        return device(x, y, lax.rem(z + i, 8), c)

    where_z = {r: (ch, zz) for ch, rs in enumerate(CHUNKS) for zz, r in enumerate(rs)}

    def z_copy(r):
        ch, zz = where_z[r]
        return remote(
            normed_ref, tok.at[ch, 0, zz * 16 : zz * 16 + 16], z_send.at[r], z_recv.at[r], at_z(r)
        )

    def half(h):
        return pl.ds(h * 1024, 1024)

    def whole():
        return pl.ds(0, D)

    def y_copy(way, t, ch):
        a, b, dev = (t, t + 1, right) if way == 0 else ((8 - t) % 8, 7 - t, left)
        cols = whole() if t < 3 else half(way)
        return remote(
            tok.at[ch, PLACE[a], :, cols], tok.at[ch, PLACE[b], :, cols],
            y_send.at[way, t, ch], y_recv.at[way, t, ch], dev,
        )

    def r_copy(way, t, ch):
        src, dst, dev = (sl, rl, left) if way == 0 else (sr, rr, right)
        cols = whole() if t > 0 else half(way)
        return remote(
            src.at[ch, t, :, cols], dst.at[ch, t, :, cols],
            r_send.at[way, t, ch], r_recv.at[way, t, ch], dev,
        )

    def x_copy(u, j):
        return remote(xs.at[u, j], xr.at[u, j], x_send.at[u, j], x_recv.at[u, j], at_x(j))

    def b_copy(u, j):
        return remote(po.at[u, j], pr.at[u, j], b_send.at[u, j], b_recv.at[u, j], at_x(j, True))

    def f_copy(r):
        ch, zz = where_z[r]
        return remote(
            fs.at[ch, zz * 16 : zz * 16 + 16], fr.at[r], f_send.at[r], f_recv.at[r], at_z(8 - r)
        )

    def gather(ch, t):
        if t == 0:
            for r in CHUNKS[ch]:
                if r:
                    z_copy(r).wait_recv()
        for way in range(2):
            if t > 0:
                y_copy(way, t - 1, ch).wait_recv()
            if t < 4:
                y_copy(way, t, ch).start()

    def select(ch, g):
        u = 2 * ch + g
        lane = lax.broadcasted_iota(jnp.int32, (16, 128), 1)
        table = jnp.zeros((16, 128), F32)
        for p in range(4):
            y0 = lax.rem(y + 8 - ORDER[4 * g + p], 8)
            for zz in range(2):
                z0 = lax.rem(z + 8 - CHUNKS[ch][zz], 8)
                n = 2 * p + zz
                rolled = pltpu.roll(table_ref[y0], lax.rem(n * 16 + 128 - z0 * 16, 128), 1)
                table = jnp.where((lane >> 4) == n, rolled, table)
        row = lax.broadcasted_iota(jnp.int32, (128, 128), 0)
        col = lax.broadcasted_iota(jnp.int32, (128, 128), 1)
        req = zhi * 8 + ((x + (row >> 5)) & 3) * 2 + ((c + (row >> 4)) & 1)
        expert = (4 * req + seq // 4).astype(F32)
        same = ((row >> 1) & 7) == (col >> 4)
        match = jnp.zeros((128, 128), F32)
        gate = jnp.zeros((128, 128), F32)
        for k in range(8):
            hit = same & (table[k : k + 1, :] == expert)
            match = jnp.where(hit, 1.0, match)
            gate = jnp.where(hit, table[8 + k : 9 + k, :], gate)
        before = jnp.where(row < col, 1.0, 0.0).astype(BF)
        rank = jnp.dot(match.astype(BF), before, preferred_element_type=F32)
        pick = jnp.where(rank == (row & 1).astype(F32), match, 0.0)
        comb[u] = (pick * gate).T.astype(BF)
        pick = pick.astype(BF)

        def tile(n, _):
            cols = pl.ds(pl.multiple_of(n * 512, 512), 512)
            rows = tok[ch, 4 * g : 4 * g + 4, :, cols].reshape(128, 512)
            rows = jnp.dot(pick, rows, preferred_element_type=F32).astype(BF)
            xs[u, :, :, cols] = rows.reshape(8, 16, 512)
            xr[u, 0, :, cols] = rows[:16]
            return 0

        lax.fori_loop(0, 4, tile, 0)

        def send(j, _):
            x_copy(u, j).start()
            return 0

        lax.fori_loop(1, 8, send, 0)

    def feed(ch, g):
        u = 2 * ch + g

        def arrive(j, _):
            x_copy(u, j).wait_recv()
            return 0

        lax.fori_loop(1, 8, arrive, 0)
        both = jnp.dot(xr[u].reshape(128, D), wg_ref[...], preferred_element_type=F32)
        v, w = both[:, :192], both[:, 192:]
        hidden = (v / (1.0 + jnp.exp(-v)) * w).astype(BF)

        def tile(n, _):
            cols = pl.ds(pl.multiple_of(n * 512, 512), 512)
            rows = jnp.dot(hidden, wd_ref[:, cols], preferred_element_type=F32).astype(BF)
            po[u, :, :, cols] = rows.reshape(8, 16, 512)
            pr[u, 0, :, cols] = rows[:16]
            return 0

        lax.fori_loop(0, 4, tile, 0)

        def send(j, _):
            b_copy(u, j).start()
            return 0

        lax.fori_loop(1, 8, send, 0)

    def combine(ch, g):
        u = 2 * ch + g

        def arrive(j, _):
            b_copy(u, j).wait_recv()
            return 0

        lax.fori_loop(1, 8, arrive, 0)

        def tile(n, _):
            cols = pl.ds(pl.multiple_of(n * 512, 512), 512)
            rows = pr[u, :, :, cols].reshape(128, 512)
            rows = jnp.dot(comb[u], rows, preferred_element_type=F32)
            part[ch, 4 * g : 4 * g + 4, :, cols] = rows.reshape(4, 32, 512)
            return 0

        lax.fori_loop(0, 4, tile, 0)

    def scatter(ch, t):
        for way in range(2):
            o = 4 - t if way == 0 else 4 + t
            src, dst = (sl, rl) if way == 0 else (sr, rr)
            if t > 0:
                r_copy(way, t - 1, ch).wait_recv()
            for h in range(2):
                if t == 0 and h != way:
                    continue
                value = part[ch, PLACE[o], :, half(h)]
                if t > 1 or (t == 1 and h == way):
                    value = value + dst[ch, t - 1, :, half(h)].astype(F32)
                src[ch, t, :, half(h)] = value.astype(BF)
            r_copy(way, t, ch).start()

    def finish(ch):
        for way in range(2):
            r_copy(way, 3, ch).wait_recv()
        for h in range(2):
            value = part[ch, 0, :, half(h)] + rl[ch, 3, :, half(h)].astype(F32)
            fs[ch, :, half(h)] = (value + rr[ch, 3, :, half(h)].astype(F32)).astype(BF)
        for r in CHUNKS[ch]:
            if r:
                f_copy(r).start()

    for r in (1, 7, 2, 6, 3, 5, 4):
        z_copy(r).start()
    tok[0, 0, :16] = normed_ref[...]

    for copy in weights:
        copy.wait()
    work = {"g": gather, "s": select, "f": feed, "c": combine, "r": scatter, "n": lambda ch, _: finish(ch)}
    for kind, ch, i in PLAN:
        work[kind](ch, i)

    acc = res_ref[...].astype(F32) + fs[0, :16].astype(F32)
    for r in (1, 7, 2, 6, 3, 5, 4):
        f_copy(r).wait_recv()
        acc = acc + fr[r].astype(F32)
    out_ref[...] = acc.astype(BF)

    for r in range(1, 8):
        z_copy(r).wait_send()
        f_copy(r).wait_send()
    for ch in range(4):
        for t in range(4):
            for way in range(2):
                y_copy(way, t, ch).wait_send()
                r_copy(way, t, ch).wait_send()

    def sent(u, _):
        def one(j, _):
            x_copy(u, j).wait_send()
            b_copy(u, j).wait_send()
            return 0

        return lax.fori_loop(1, 8, one, 0)

    lax.fori_loop(0, 8, sent, 0)


def layer_kernel(counts, *refs):
    groups, at = [], 0
    for n in counts:
        groups.append(refs[at : at + n])
        at += n
    ins, (wg_hbm, wd_hbm, out_ref), middle, (wg, wd, w_sem), first, second = groups
    weights = [
        pltpu.make_async_copy(wg_hbm, wg, w_sem.at[0]),
        pltpu.make_async_copy(wd_hbm, wd, w_sem.at[1]),
    ]
    res, normed, table = middle
    attention_part(weights, *ins, res, normed, table, *first)
    experts_part(weights, normed, res, table, wg, wd, out_ref, *second)


def layer(cached_len, kv, q, wt, x, gain, mark, wg, wd):
    vm = pl.BlockSpec(memory_space=pltpu.VMEM)
    anywhere = pl.BlockSpec(memory_space=pl.ANY)
    dma = pltpu.SemaphoreType.DMA
    big = pltpu.VMEM((8, 8, 16, D), BF)
    hop = pltpu.VMEM((4, 4, 32, D), BF)
    middle = [pltpu.VMEM((16, D), BF), pltpu.VMEM((16, D), BF), pltpu.VMEM((8, 16, 128), F32)]
    held = [pltpu.VMEM(wg.shape, BF), pltpu.VMEM(wd.shape, BF), dma((2,))]
    first = [
            pltpu.VMEM((16, 16, 128), F32),
            pltpu.VMEM((8, 16, 128), F32),
            pltpu.VMEM((4, 8, 16, 128), F32),
            pltpu.VMEM((2048, HD), BF),
            pltpu.VMEM((2048, HD), BF),
            pltpu.VMEM((256, 256), BF),
            pltpu.VMEM((16, 2, 64, 256), BF),
            pltpu.VMEM((256, 256), BF),
            pltpu.VMEM((256, D), BF),
            pltpu.VMEM((16, 16, D), BF),
            dma((16,)), dma((16,)),
            dma((4,)), dma((4,)),
            dma((5,)),
            dma((3, 16)), dma((3, 16)),
            dma((16,)), dma((16,)),
            dma, dma,
            dma((16,)), dma((16,)),
    ]
    second = [
            pltpu.VMEM((4, 8, 32, D), BF),
            pltpu.VMEM((8, 128, 128), BF),
            big, big, big, big,
            pltpu.VMEM((4, 8, 32, D), F32),
            hop, hop, hop, hop,
            pltpu.VMEM((4, 32, D), BF),
            pltpu.VMEM((8, 16, D), BF),
            dma((8,)), dma((8,)),
            dma((2, 4, 4)), dma((2, 4, 4)),
            dma((8, 8)), dma((8, 8)),
            dma((8, 8)), dma((8, 8)),
            dma((2, 4, 4)), dma((2, 4, 4)),
            dma((8,)), dma((8,)),
    ]
    counts = (7, 3, 3, 3, len(first), len(second))
    return pl.pallas_call(
        functools.partial(layer_kernel, counts),
        name="layer",
        out_shape=jax.ShapeDtypeStruct((16, D), BF),
        in_specs=[pl.BlockSpec(memory_space=pltpu.SMEM)] + [vm] * 6 + [anywhere] * 2,
        out_specs=vm,
        scratch_shapes=middle + held + first + second,
        compiler_params=pltpu.CompilerParams(
            collective_id=0, has_side_effects=True, vmem_limit_bytes=60 * 1024 * 1024
        ),
    )(cached_len, kv, q, wt, x, gain, mark, wg, wd)


def local(
    layer_input, queries, fresh_kv, cache_kv, cached_len, out_weight, norm_gain,
    routes, route_gates, w_gate_up, w_down,
):
    z = coords()[2]
    mark = jnp.concatenate([routes[0].T.astype(F32), route_gates[0].T], 0)
    mark = jnp.where(jnp.arange(128)[None] // 16 == z, jnp.tile(mark, (1, 8)), 0.0)
    kv = jnp.concatenate([cache_kv[0], fresh_kv[0]], 0)
    out = layer(
        cached_len, kv, queries[0], out_weight.T, layer_input[0], norm_gain[None], mark,
        w_gate_up[0], w_down[0],
    )
    return out[None]


def solution(mesh):
    return jax.shard_map(
        local,
        mesh=mesh,
        in_specs=(
            P("req", "seq", None),
            P("req", "seq", None),
            P("req", "seq", None),
            P("req", "seq", None),
            P("req"),
            P("seq", "req"),
            P(),
            P("req", "seq", None),
            P("req", "seq", None),
            P(("req", "seq"), None, None),
            P(("req", "seq"), None, None),
        ),
        out_specs=P("req", "seq", None),
        check_vma=False,
    )
```

```python
import functools
import math

import jax
import jax.numpy as jnp
from jax import lax
from jax.experimental import pallas as pl
from jax.experimental.pallas import tpu as pltpu
from jax.sharding import PartitionSpec as P

MESH = pl.DeviceIdType.MESH
BF = jnp.bfloat16
F32 = jnp.float32
NEG = -1e30
EPS = 1e-06
D = 2048
HD = 128
NT = (((1,), (1,)), ((), ()))


def coords():
    req, seq = lax.axis_index("req"), lax.axis_index("seq")
    z = (req // 8) * 2 + seq // 8
    return (req // 2) % 4, seq % 8, z, req % 2


def device(x, y, z, c):
    return ((z // 2) * 8 + x * 2 + c, (z % 2) * 8 + y)


def remote(src, dst, send, recv, dev):
    return pltpu.make_async_remote_copy(
        src_ref=src, dst_ref=dst, send_sem=send, recv_sem=recv, device_id=dev, device_id_type=MESH
    )


def greet(devs):
    barrier = pltpu.get_barrier_semaphore()
    for dev in devs:
        pl.semaphore_signal(barrier, inc=1, device_id=dev, device_id_type=MESH)
    pl.semaphore_wait(barrier, len(devs))


def attention_part(
    weights, len_ref, kv_ref, q_ref, wt_ref, x_ref, gain_ref, routes_ref, gates_ref, res_ref, normed_ref, table_ref,
    mark_ref, marks, near, far, kbuf, vbuf, qbuf, wbuf, att, pbuf, rbuf,
    m_send, m_recv, n_send, n_recv, own_sem, kv_send, kv_recv, w_send, w_recv, sib_send, sib_recv, p_send, p_recv,
):
    req, seq = lax.axis_index("req"), lax.axis_index("seq")
    m, c = req // 2, req % 2
    peers = [(req, lax.rem(seq + i, 16)) for i in range(1, 16)]
    chips = [(lax.rem(m + i, 16) * 2 + c, seq) for i in range(1, 16)]
    sibling = (m * 2 + 1 - c, seq)
    x, y, z, _ = coords()
    row = lax.broadcasted_iota(jnp.int32, (16, 128), 0)
    place = lax.broadcasted_iota(jnp.int32, (16, 128), 1) == row + z * 16
    place = jnp.where(place, 1.0, 0.0).astype(BF)
    both = jnp.concatenate([routes_ref[...].astype(F32), gates_ref[...]], 0).astype(BF)
    mark_ref[...] = jnp.dot(both, place, preferred_element_type=F32)
    across = [device(lax.rem(x + i, 4), y, z, 1 - c) for i in range(1, 4)]
    along = [device(x, y, lax.rem(z + i, 8), c) for i in range(1, 8)]
    greet(peers + chips + [sibling] + across + along)
    for copy in weights:
        copy.start()

    def piece(part, dst_seq, src_seq, i):
        rows = pl.ds(pl.multiple_of(src_seq * 128, 128), 128)
        head = dst_seq // 4
        if part == 0:
            cols = pl.ds(pl.multiple_of(head * HD, HD), HD)
            return kv_ref.at[:, cols], kbuf.at[rows, :]
        if part == 1:
            cols = pl.ds(pl.multiple_of(512 + head * HD, HD), HD)
            return kv_ref.at[:, cols], vbuf.at[rows, :]
        rows = pl.ds(pl.multiple_of(src_seq * 16, 16), 16)
        cols = pl.ds(pl.multiple_of(dst_seq * 256, 256), 256)
        return q_ref.at[:, cols], qbuf.at[rows, :]

    def kv_copy(part, i):
        dst_seq = lax.rem(seq + i, 16)
        src, dst = piece(part, dst_seq, seq, i)
        return remote(src, dst, kv_send.at[part, i], kv_recv.at[part, i], (req, dst_seq))

    def w_copy(i):
        return remote(
            wt_ref, wbuf.at[m, c], w_send.at[i], w_recv.at[i], (lax.rem(m + i, 16) * 2 + c, seq)
        )

    def mark_copy(i):
        dst_seq = lax.rem(seq + i, 16)
        return remote(mark_ref, marks.at[seq], m_send.at[i], m_recv.at[i], (req, dst_seq))

    def near_copy(i):
        dst = (lax.rem(req + 8 * i, 32), seq)
        return remote(near, far.at[i], n_send.at[i], n_recv.at[i], dst)

    def mark_wait(i, _):
        mark_copy(i).wait()
        return 0

    def start(i, _):
        mark_copy(i).start()
        for part in range(3):
            kv_copy(part, i).start()
        w_copy(i).start()
        return 0

    lax.fori_loop(1, 16, start, 0)
    own = []
    for part in range(3):
        src, dst = piece(part, seq, seq, 0)
        own.append(pltpu.make_async_copy(src, dst, own_sem.at[part]))
    own.append(pltpu.make_async_copy(wt_ref, wbuf.at[m, c], own_sem.at[3]))
    own.append(pltpu.make_async_copy(mark_ref, marks.at[seq], own_sem.at[4]))
    for copy in own:
        copy.start()
    for copy in own:
        copy.wait()

    def kv_wait(i, _):
        for part in range(3):
            kv_copy(part, i).wait()
        return 0

    def w_wait(i, _):
        w_copy(i).wait()
        return 0

    lax.fori_loop(1, 16, mark_wait, 0)
    for n in range(8):
        near[n] = marks[n] + marks[8 + n]
    for i in range(1, 4):
        near_copy(i).start()
    lax.fori_loop(1, 16, w_wait, 0)
    sib = remote(wbuf.at[:, c], wbuf.at[:, c], sib_send, sib_recv, sibling)
    sib.start()
    lax.fori_loop(1, 16, kv_wait, 0)

    length = len_ref[0]
    scale = 1.0 / math.sqrt(HD)
    sib.wait()

    def p_copy(dst_seq):
        i = lax.rem(dst_seq + 16 - seq, 16)
        rows = pl.ds(pl.multiple_of(dst_seq * 16, 16), 16)
        return remote(pbuf.at[rows, :], rbuf.at[i], p_send.at[i], p_recv.at[i], (req, dst_seq))

    def tile(step, _):
        quad = lax.rem(seq // 4 + 1 + step, 4)
        rows = pl.ds(pl.multiple_of(quad * 64, 64), 64)
        for head in range(2):
            q = qbuf[rows, head * HD : (head + 1) * HD]
            s = lax.dot_general(q, kbuf[...], NT, preferred_element_type=F32) * scale
            col = lax.broadcasted_iota(jnp.int32, (64, D), 1)
            tok = lax.broadcasted_iota(jnp.int32, (64, D), 0) + quad * 64
            src, within = col >> 7, col & 127
            behind = jnp.where(
                within < 112, src * 112 + within - length, src * 16 + within - 113 - tok
            )
            seen = behind < 0
            s = jnp.where(seen, s, NEG)
            w = jnp.where(seen, jnp.exp(s - jnp.max(s, axis=-1, keepdims=True)), 0.0)
            total = jnp.sum(w, axis=-1, keepdims=True)
            mixed = jnp.dot(w.astype(BF), vbuf[...], preferred_element_type=F32)
            att[rows, head * HD : (head + 1) * HD] = (mixed / total).astype(BF)

        def project(i, _):
            w = wbuf[pl.ds(i * 4, 4)].reshape(512, 256)
            cols = pl.ds(pl.multiple_of(i * 512, 512), 512)
            out = lax.dot_general(att[rows, :], w, NT, preferred_element_type=F32)
            pbuf[rows, cols] = out.astype(BF)
            return 0

        lax.fori_loop(0, 4, project, 0)

        def send(n, _):
            dst_seq = quad * 4 + lax.rem(seq + n, 4)

            @pl.when(dst_seq != seq)
            def _():
                p_copy(dst_seq).start()

            return 0

        return lax.fori_loop(0, 4, send, 0)

    lax.fori_loop(0, 4, tile, 0)

    def p_wait(i, _):
        p_copy(lax.rem(seq + i, 16)).wait()
        return 0

    for i in range(1, 4):
        near_copy(i).wait()
    for n in range(8):
        table_ref[n] = near[n] + far[1, n] + far[2, n] + far[3, n]
    rbuf[0] = pbuf[pl.ds(pl.multiple_of(seq * 16, 16), 16), :]
    lax.fori_loop(1, 16, p_wait, 0)
    projected = lax.fori_loop(
        0, 16, lambda i, acc: acc + rbuf[i].astype(F32), jnp.zeros((16, D), F32)
    )
    residual = (x_ref[...].astype(F32) + projected).astype(BF)
    res_ref[...] = residual
    r = residual.astype(F32)
    mean = jnp.mean(r * r, axis=-1, keepdims=True)
    normed_ref[...] = (r * lax.rsqrt(mean + EPS) * gain_ref[...]).astype(BF)


ORDER = (0, 1, 7, 2, 6, 3, 5, 4)
PLACE = {o: i for i, o in enumerate(ORDER)}
CHUNKS = ((0, 1), (7, 2), (6, 3), (5, 4))

PLAN = (
    ("g", 0, 0),
    ("g", 1, 0),
    ("g", 0, 1),
    ("g", 1, 1),
    ("g", 0, 2),
    ("s", 0, 0),
    ("g", 1, 2),
    ("g", 2, 0),
    ("s", 1, 0),
    ("g", 1, 3),
    ("g", 0, 3),
    ("g", 3, 0),
    ("f", 0, 0),
    ("g", 1, 4),
    ("g", 0, 4),
    ("g", 2, 1),
    ("s", 0, 1),
    ("g", 3, 1),
    ("g", 2, 2),
    ("s", 1, 1),
    ("g", 2, 3),
    ("f", 0, 1),
    ("f", 1, 1),
    ("g", 2, 4),
    ("c", 0, 1),
    ("g", 3, 2),
    ("s", 2, 1),
    ("g", 3, 3),
    ("f", 1, 0),
    ("c", 1, 1),
    ("s", 2, 0),
    ("r", 0, 0),
    ("g", 3, 4),
    ("r", 1, 0),
    ("s", 3, 1),
    ("c", 1, 0),
    ("r", 0, 1),
    ("c", 0, 0),
    ("r", 1, 1),
    ("s", 3, 0),
    ("f", 3, 1),
    ("r", 0, 2),
    ("r", 1, 2),
    ("f", 2, 1),
    ("f", 3, 0),
    ("r", 1, 3),
    ("f", 2, 0),
    ("c", 3, 1),
    ("r", 3, 0),
    ("r", 0, 3),
    ("c", 2, 1),
    ("r", 2, 0),
    ("r", 3, 1),
    ("n", 1, 0),
    ("r", 2, 1),
    ("c", 3, 0),
    ("r", 3, 2),
    ("c", 2, 0),
    ("r", 2, 2),
    ("r", 3, 3),
    ("r", 2, 3),
    ("n", 0, 0),
    ("n", 3, 0),
    ("n", 2, 0),
)


def experts_part(
    weights, normed_ref, res_ref, table_ref, wg_ref, wd_ref, out_ref,
    tok, comb, xs, xr, po, pr, part, sl, rl, sr, rr, fs, fr,
    z_send, z_recv, y_send, y_recv, x_send, x_recv, b_send, b_recv, r_send, r_recv, f_send, f_recv,
):
    x, y, z, c = coords()
    seq, zhi = (z % 2) * 8 + y, z // 2
    right, left = device(x, lax.rem(y + 1, 8), z, c), device(x, lax.rem(y + 7, 8), z, c)

    def at_x(j, back=False):
        far = 4 - j // 2 if back else j // 2
        return device(lax.rem(x + far, 4), y, z, lax.rem(c + j, 2))

    def at_z(i):
        return device(x, y, lax.rem(z + i, 8), c)

    where_z = {r: (ch, zz) for ch, rs in enumerate(CHUNKS) for zz, r in enumerate(rs)}

    def z_copy(r):
        ch, zz = where_z[r]
        return remote(
            normed_ref, tok.at[ch, 0, zz * 16 : zz * 16 + 16], z_send.at[r], z_recv.at[r], at_z(r)
        )

    def half(h):
        return pl.ds(h * 1024, 1024)

    def whole():
        return pl.ds(0, D)

    def y_copy(way, t, ch):
        a, b, dev = (t, t + 1, right) if way == 0 else ((8 - t) % 8, 7 - t, left)
        cols = whole() if t < 3 else half(way)
        return remote(
            tok.at[ch, PLACE[a], :, cols], tok.at[ch, PLACE[b], :, cols],
            y_send.at[way, t, ch], y_recv.at[way, t, ch], dev,
        )

    def r_copy(way, t, ch):
        src, dst, dev = (sl, rl, left) if way == 0 else (sr, rr, right)
        cols = whole() if t > 0 else half(way)
        return remote(
            src.at[ch, t, :, cols], dst.at[ch, t, :, cols],
            r_send.at[way, t, ch], r_recv.at[way, t, ch], dev,
        )

    def x_copy(u, j):
        return remote(xs.at[u, j], xr.at[u, j], x_send.at[u, j], x_recv.at[u, j], at_x(j))

    def b_copy(u, j):
        return remote(po.at[u, j], pr.at[u, j], b_send.at[u, j], b_recv.at[u, j], at_x(j, True))

    def f_copy(r):
        ch, zz = where_z[r]
        return remote(
            fs.at[ch, zz * 16 : zz * 16 + 16], fr.at[r], f_send.at[r], f_recv.at[r], at_z(8 - r)
        )

    def gather(ch, t):
        if t == 0:
            for r in CHUNKS[ch]:
                if r:
                    z_copy(r).wait_recv()
        for way in range(2):
            if t > 0:
                y_copy(way, t - 1, ch).wait_recv()
            if t < 4:
                y_copy(way, t, ch).start()

    def select(ch, g):
        u = 2 * ch + g
        lane = lax.broadcasted_iota(jnp.int32, (16, 128), 1)
        table = jnp.zeros((16, 128), F32)
        for p in range(4):
            y0 = lax.rem(y + 8 - ORDER[4 * g + p], 8)
            for zz in range(2):
                z0 = lax.rem(z + 8 - CHUNKS[ch][zz], 8)
                n = 2 * p + zz
                rolled = pltpu.roll(table_ref[y0], lax.rem(n * 16 + 128 - z0 * 16, 128), 1)
                table = jnp.where((lane >> 4) == n, rolled, table)
        row = lax.broadcasted_iota(jnp.int32, (128, 128), 0)
        col = lax.broadcasted_iota(jnp.int32, (128, 128), 1)
        req = zhi * 8 + ((x + (row >> 5)) & 3) * 2 + ((c + (row >> 4)) & 1)
        expert = (4 * req + seq // 4).astype(F32)
        same = ((row >> 1) & 7) == (col >> 4)
        match = jnp.zeros((128, 128), F32)
        gate = jnp.zeros((128, 128), F32)
        for k in range(8):
            hit = same & (table[k : k + 1, :] == expert)
            match = jnp.where(hit, 1.0, match)
            gate = jnp.where(hit, table[8 + k : 9 + k, :], gate)
        before = jnp.where(row < col, 1.0, 0.0).astype(BF)
        rank = jnp.dot(match.astype(BF), before, preferred_element_type=F32)
        pick = jnp.where(rank == (row & 1).astype(F32), match, 0.0)
        comb[u] = (pick * gate).T.astype(BF)
        pick = pick.astype(BF)

        def tile(n, _):
            cols = pl.ds(pl.multiple_of(n * 512, 512), 512)
            rows = tok[ch, 4 * g : 4 * g + 4, :, cols].reshape(128, 512)
            rows = jnp.dot(pick, rows, preferred_element_type=F32).astype(BF)
            xs[u, :, :, cols] = rows.reshape(8, 16, 512)
            xr[u, 0, :, cols] = rows[:16]
            return 0

        lax.fori_loop(0, 4, tile, 0)

        def send(j, _):
            x_copy(u, j).start()
            return 0

        lax.fori_loop(1, 8, send, 0)

    def feed(ch, g):
        u = 2 * ch + g

        def arrive(j, _):
            x_copy(u, j).wait_recv()
            return 0

        lax.fori_loop(1, 8, arrive, 0)
        both = jnp.dot(xr[u].reshape(128, D), wg_ref[...], preferred_element_type=F32)
        v, w = both[:, :192], both[:, 192:]
        hidden = (v / (1.0 + jnp.exp(-v)) * w).astype(BF)

        def tile(n, _):
            cols = pl.ds(pl.multiple_of(n * 512, 512), 512)
            rows = jnp.dot(hidden, wd_ref[:, cols], preferred_element_type=F32).astype(BF)
            po[u, :, :, cols] = rows.reshape(8, 16, 512)
            pr[u, 0, :, cols] = rows[:16]
            return 0

        lax.fori_loop(0, 4, tile, 0)

        def send(j, _):
            b_copy(u, j).start()
            return 0

        lax.fori_loop(1, 8, send, 0)

    def combine(ch, g):
        u = 2 * ch + g

        def arrive(j, _):
            b_copy(u, j).wait_recv()
            return 0

        lax.fori_loop(1, 8, arrive, 0)

        def tile(n, _):
            cols = pl.ds(pl.multiple_of(n * 512, 512), 512)
            rows = pr[u, :, :, cols].reshape(128, 512)
            rows = jnp.dot(comb[u], rows, preferred_element_type=F32)
            part[ch, 4 * g : 4 * g + 4, :, cols] = rows.reshape(4, 32, 512)
            return 0

        lax.fori_loop(0, 4, tile, 0)

    def scatter(ch, t):
        for way in range(2):
            o = 4 - t if way == 0 else 4 + t
            src, dst = (sl, rl) if way == 0 else (sr, rr)
            if t > 0:
                r_copy(way, t - 1, ch).wait_recv()
            for h in range(2):
                if t == 0 and h != way:
                    continue
                value = part[ch, PLACE[o], :, half(h)]
                if t > 1 or (t == 1 and h == way):
                    value = value + dst[ch, t - 1, :, half(h)].astype(F32)
                src[ch, t, :, half(h)] = value.astype(BF)
            r_copy(way, t, ch).start()

    def finish(ch):
        for way in range(2):
            r_copy(way, 3, ch).wait_recv()
        for h in range(2):
            value = part[ch, 0, :, half(h)] + rl[ch, 3, :, half(h)].astype(F32)
            fs[ch, :, half(h)] = (value + rr[ch, 3, :, half(h)].astype(F32)).astype(BF)
        for r in CHUNKS[ch]:
            if r:
                f_copy(r).start()

    for r in (1, 7, 2, 6, 3, 5, 4):
        z_copy(r).start()
    tok[0, 0, :16] = normed_ref[...]

    for copy in weights:
        copy.wait()
    work = {"g": gather, "s": select, "f": feed, "c": combine, "r": scatter, "n": lambda ch, _: finish(ch)}
    for kind, ch, i in PLAN:
        work[kind](ch, i)

    acc = res_ref[...].astype(F32) + fs[0, :16].astype(F32)
    for r in (1, 7, 2, 6, 3, 5, 4):
        f_copy(r).wait_recv()
        acc = acc + fr[r].astype(F32)
    out_ref[...] = acc.astype(BF)

    for r in range(1, 8):
        z_copy(r).wait_send()
        f_copy(r).wait_send()
    for ch in range(4):
        for t in range(4):
            for way in range(2):
                y_copy(way, t, ch).wait_send()
                r_copy(way, t, ch).wait_send()

    def sent(u, _):
        def one(j, _):
            x_copy(u, j).wait_send()
            b_copy(u, j).wait_send()
            return 0

        return lax.fori_loop(1, 8, one, 0)

    lax.fori_loop(0, 8, sent, 0)


def layer_kernel(counts, *refs):
    groups, at = [], 0
    for n in counts:
        groups.append(refs[at : at + n])
        at += n
    ins, (wg_hbm, wd_hbm, out_ref), middle, (wg, wd, w_sem), first, second = groups
    weights = [
        pltpu.make_async_copy(wg_hbm, wg, w_sem.at[0]),
        pltpu.make_async_copy(wd_hbm, wd, w_sem.at[1]),
    ]
    res, normed, table = middle
    attention_part(weights, *ins, res, normed, table, *first)
    experts_part(weights, normed, res, table, wg, wd, out_ref, *second)


def layer(cached_len, kv, q, wt, x, gain, routes, gates, wg, wd):
    vm = pl.BlockSpec(memory_space=pltpu.VMEM)
    anywhere = pl.BlockSpec(memory_space=pl.ANY)
    dma = pltpu.SemaphoreType.DMA
    big = pltpu.VMEM((8, 8, 16, D), BF)
    hop = pltpu.VMEM((4, 4, 32, D), BF)
    middle = [pltpu.VMEM((16, D), BF), pltpu.VMEM((16, D), BF), pltpu.VMEM((8, 16, 128), F32)]
    held = [pltpu.VMEM(wg.shape, BF), pltpu.VMEM(wd.shape, BF), dma((2,))]
    first = [
            pltpu.VMEM((16, 128), F32),
            pltpu.VMEM((16, 16, 128), F32),
            pltpu.VMEM((8, 16, 128), F32),
            pltpu.VMEM((4, 8, 16, 128), F32),
            pltpu.VMEM((2048, HD), BF),
            pltpu.VMEM((2048, HD), BF),
            pltpu.VMEM((256, 256), BF),
            pltpu.VMEM((16, 2, 64, 256), BF),
            pltpu.VMEM((256, 256), BF),
            pltpu.VMEM((256, D), BF),
            pltpu.VMEM((16, 16, D), BF),
            dma((16,)), dma((16,)),
            dma((4,)), dma((4,)),
            dma((5,)),
            dma((3, 16)), dma((3, 16)),
            dma((16,)), dma((16,)),
            dma, dma,
            dma((16,)), dma((16,)),
    ]
    second = [
            pltpu.VMEM((4, 8, 32, D), BF),
            pltpu.VMEM((8, 128, 128), BF),
            big, big, big, big,
            pltpu.VMEM((4, 8, 32, D), F32),
            hop, hop, hop, hop,
            pltpu.VMEM((4, 32, D), BF),
            pltpu.VMEM((8, 16, D), BF),
            dma((8,)), dma((8,)),
            dma((2, 4, 4)), dma((2, 4, 4)),
            dma((8, 8)), dma((8, 8)),
            dma((8, 8)), dma((8, 8)),
            dma((2, 4, 4)), dma((2, 4, 4)),
            dma((8,)), dma((8,)),
    ]
    counts = (8, 3, 3, 3, len(first), len(second))
    return pl.pallas_call(
        functools.partial(layer_kernel, counts),
        name="layer",
        out_shape=jax.ShapeDtypeStruct((16, D), BF),
        in_specs=[pl.BlockSpec(memory_space=pltpu.SMEM)] + [vm] * 7 + [anywhere] * 2,
        out_specs=vm,
        scratch_shapes=middle + held + first + second,
        compiler_params=pltpu.CompilerParams(
            collective_id=0, has_side_effects=True, vmem_limit_bytes=60 * 1024 * 1024
        ),
    )(cached_len, kv, q, wt, x, gain, routes, gates, wg, wd)


def local(
    layer_input, queries, fresh_kv, cache_kv, cached_len, out_weight, norm_gain,
    routes, route_gates, w_gate_up, w_down,
):
    kv = jnp.concatenate([cache_kv[0], fresh_kv[0]], 0)
    out = layer(
        cached_len, kv, queries[0], out_weight.T, layer_input[0], norm_gain[None],
        routes[0].T, route_gates[0].T, w_gate_up[0], w_down[0],
    )
    return out[None]


def solution(mesh):
    return jax.shard_map(
        local,
        mesh=mesh,
        in_specs=(
            P("req", "seq", None),
            P("req", "seq", None),
            P("req", "seq", None),
            P("req", "seq", None),
            P("req"),
            P("seq", "req"),
            P(),
            P("req", "seq", None),
            P("req", "seq", None),
            P(("req", "seq"), None, None),
            P(("req", "seq"), None, None),
        ),
        out_specs=P("req", "seq", None),
        check_vma=False,
    )
```
